256 devices in a mesh: patch: 32 (over z, y_lo, core), lev: 8 (over y_hi, x).
Axes of the slice: x: 4, y: 4 (y_hi: 2, y_lo: 2; y = y_hi * 2 + y_lo), z: 8, core: 2. Of those that a mesh axis runs over, the one named last changes fastest.
Arguments:
- fields: float32 [3, 96, 65536], P(None, 'lev', 'patch'), may hold values from -6 to 6
- stencil_index: int32 [12, 8, 65536], P(None, 'lev', 'patch'), may hold values from 0 to 3071, as said below
- stencil_weight: float32 [12, 8, 65536], P(None, 'lev', 'patch'), may hold values from -0.2 to 0.4
- neighbours: int32 [6, 65536], P(None, 'patch'), may hold values from 0 to 2175, as said below
- lap_weight: float32 [6, 65536], P(None, 'patch'), may hold values from 0.2 to 1
- edge_x: float32 [6, 65536], P(None, 'patch'), may hold values from -1.8 to 1.8
- edge_y: float32 [6, 65536], P(None, 'patch'), may hold values from -1.8 to 1.8
- to_modes: float32 [96, 96], replicated, may hold values from -0.625 to 0.625
- from_modes: float32 [96, 96], replicated, may hold values from -0.625 to 0.625
- helm_coef: float32 [96], P('lev'), may hold values from 0.15 to 0.6
Outputs:
- new_winds: float32 [2, 96, 65536], P(None, 'lev', 'patch')
- new_height: float32 [96, 65536], P('lev', 'patch')
The draws below stay inside these ranges and needn't reach their ends.
Inputs may be any that keep to these rules, and one draw needn't show every extreme that they name: `stencil_index`: entry [p, g, i] is a position in the cells of i's patch extended by 512 cells on each side along the closed chain; position 512 + (i mod 2048) is cell i itself, and the entry lies at most 512 from it. `neighbours`: entry [k, i] is a position in the cells of i's patch extended by 64 cells on each side along the closed chain; position 64 + (i mod 2048) is cell i itself, which is never named.
All inputs are finite; a program needn't handle non-finite values.
Results may differ from the reference program's by a relative error of at most 0.000096.
Values sent between devices are 32-bit elements; how exact they have to be, the bound alone decides.
No kernel may reach another device: no remote copies, remote signals or barrier semaphores. Data moves between devices by JAX's collectives and lax.ppermute only.
A program may use at most 64 MiB of HBM per device.

```python
import math
import jax
import jax.numpy as jnp
from jax import lax

CELLS_DEV = 2048
LEV_DEV = 12
REACH = 512
NBR_REACH = 64
SWEEPS = 4
LEVELS = 96
GROUPS = 8
NCELLS = 65536


def draw_stencil_index(key, part):
    key_reach = jax.random.fold_in(key, 11)
    key_group = jax.random.fold_in(key, 12)
    key_patch = jax.random.fold_in(key, 13)
    key_shift = jax.random.fold_in(key, 14)
    key_spread = jax.random.fold_in(key, 15)
    patches = NCELLS // CELLS_DEV
    reach_block = jax.random.randint(key_reach, (GROUPS, patches), 4, REACH + 1)
    group_pick = jax.random.randint(key_group, (), 0, GROUPS)
    patch_pick = jax.random.randint(key_patch, (), 0, patches)
    reach_block = reach_block.at[group_pick, patch_pick].set(REACH)
    reach_cell = jnp.repeat(reach_block, CELLS_DEV, axis=1)
    centre = REACH + jnp.arange(NCELLS, dtype=jnp.int32) % CELLS_DEV
    displace = jax.random.randint(key_shift, (GROUPS, NCELLS), -(reach_cell - 3), reach_cell - 2)
    spread = jax.random.randint(key_spread, (12, GROUPS, NCELLS), -3, 4)
    position = centre[None, None, :] + displace[None] + spread
    position = jnp.clip(position, centre[None, None, :] - reach_cell[None], centre[None, None, :] + reach_cell[None])
    first_cell = patch_pick * CELLS_DEV
    position = position.at[0, group_pick, first_cell].set(0)
    position = position.at[1, group_pick, first_cell + CELLS_DEV - 1].set(2 * REACH + CELLS_DEV - 1)
    return position.astype(jnp.int32)


def draw_neighbours(key, part):
    key_distance = jax.random.fold_in(key, 21)
    key_direction = jax.random.fold_in(key, 22)
    key_patch = jax.random.fold_in(key, 23)
    patches = NCELLS // CELLS_DEV
    distance = jax.random.randint(key_distance, (6, NCELLS), 1, NBR_REACH + 1)
    direction = jax.random.randint(key_direction, (6, NCELLS), 0, 2) * 2 - 1
    centre = NBR_REACH + jnp.arange(NCELLS, dtype=jnp.int32) % CELLS_DEV
    position = centre[None, :] + direction * distance
    patch_pick = jax.random.randint(key_patch, (), 0, patches)
    first_cell = patch_pick * CELLS_DEV
    position = position.at[0, first_cell].set(0)
    position = position.at[1, first_cell + CELLS_DEV - 1].set(2 * NBR_REACH + CELLS_DEV - 1)
    return position.astype(jnp.int32)


def steps_of(key, dims, cuts, least, high):
    factor_of, own = 1.0, jax.random.fold_in(key, 6)
    for dim, blocks in cuts:
        steps = jnp.exp(jax.random.uniform(jax.random.fold_in(own, dim), (blocks,), jnp.float32, least / len(cuts), high / len(cuts)))
        factor_of = factor_of * jnp.repeat(steps, dims[dim] // blocks).reshape([-1 if axis == dim else 1 for axis in range(len(dims))])
    return factor_of


def gaussian(rng, shape, scale, most, shards=(), held_as=jnp.bfloat16):
    loudness = steps_of(rng, shape, shards, -0.22, 0.18) if shards else 1.0
    drawn = jax.random.normal(rng, shape, jnp.float32) * scale * loudness
    return jnp.minimum(jnp.maximum(drawn, -most), most).astype(held_as)


def setup_inputs(seed: int = 0) -> dict:
    splits = jax.random.split(jax.random.key(seed), 11)
    fields = gaussian(splits[0], (3, LEVELS, NCELLS), 1.0, 6.0, ((1, 8), (2, 32)), jnp.float32)
    stencil_index = draw_stencil_index(jax.random.fold_in(splits[10], 71), 0)
    stencil_weight = jnp.clip(-0.2 + 0.6 * jax.random.uniform(splits[2], (12, GROUPS, NCELLS), jnp.float32) ** steps_of(splits[2], (12, GROUPS, NCELLS), ((1, 8), (2, 32)), -0.2, 0.2), -0.2, 0.4)
    neighbours = draw_neighbours(jax.random.fold_in(splits[10], 71), 0)
    lap_weight = jnp.clip(0.2 + 0.8 * jax.random.uniform(splits[4], (6, NCELLS), jnp.float32) ** steps_of(splits[4], (6, NCELLS), ((1, 32),), -0.2, 0.2), 0.2, 1.0)
    edge_x = gaussian(splits[5], (6, NCELLS), 0.3, 1.8, ((1, 32),), jnp.float32)
    edge_y = gaussian(splits[6], (6, NCELLS), 0.3, 1.8, ((1, 32),), jnp.float32)
    to_modes = gaussian(splits[7], (LEVELS, LEVELS), LEVELS ** -0.5, 0.625, (), jnp.float32)
    from_modes = gaussian(splits[8], (LEVELS, LEVELS), LEVELS ** -0.5, 0.625, (), jnp.float32)
    helm_coef = jnp.clip(jnp.exp(math.log(0.6) - 1.3862944 * jax.random.uniform(splits[9], (LEVELS,), jnp.float32) ** steps_of(splits[9], (LEVELS,), ((0, 8),), -0.2, 0.2)), 0.15, 0.6)
    return dict(fields=fields, stencil_index=stencil_index, stencil_weight=stencil_weight, neighbours=neighbours, lap_weight=lap_weight, edge_x=edge_x, edge_y=edge_y, to_modes=to_modes, from_modes=from_modes, helm_coef=helm_coef)


coupling = 0.5


def reference(fields, stencil_index, stencil_weight, neighbours, lap_weight, edge_x, edge_y, to_modes, from_modes, helm_coef):
    cell_ids = jnp.arange(NCELLS, dtype=jnp.int32)
    block_start = (cell_ids // CELLS_DEV) * CELLS_DEV
    source = (block_start + stencil_index - REACH) % NCELLS
    grouped = fields.reshape(3, GROUPS, LEV_DEV, NCELLS)
    upstream = jnp.zeros((3, GROUPS, LEV_DEV, NCELLS), jnp.float32)
    for point_no in range(12):
        taken = jnp.take_along_axis(grouped, source[point_no][None, :, None, :].astype(jnp.int32), axis=3)
        upstream = upstream + stencil_weight[point_no][None, :, None, :] * taken
    upstream = upstream.reshape(3, LEVELS, NCELLS)
    new_winds = upstream[0:2]
    beside_ids = (block_start + neighbours - NBR_REACH) % NCELLS
    divergence = jnp.zeros((LEVELS, NCELLS), jnp.float32)
    for slot_no in range(6):
        across = upstream[0][:, beside_ids[slot_no]] - upstream[0]
        along = upstream[1][:, beside_ids[slot_no]] - upstream[1]
        divergence = divergence + edge_x[slot_no] * across + edge_y[slot_no] * along
    right_side = upstream[2] - coupling * divergence
    modal_rhs = jnp.dot(to_modes, right_side, precision=lax.Precision.HIGHEST, preferred_element_type=jnp.float32)
    stiffness = helm_coef[:, None]
    weight_sum = jnp.sum(lap_weight, axis=0)
    diagonal = 1.0 + stiffness * weight_sum[None, :]
    radius = 6.0 * stiffness / (1.0 + 6.0 * stiffness)
    iterate = jnp.zeros((LEVELS, NCELLS), jnp.float32)
    for sweep_no in range(SWEEPS):
        step_size = 1.0 / (1.0 + radius * jnp.cos(jnp.pi * (2 * sweep_no + 1) / (2.0 * SWEEPS)))
        laplace = jnp.zeros((LEVELS, NCELLS), jnp.float32)
        for slot_no in range(6):
            laplace = laplace + lap_weight[slot_no] * (iterate[:, beside_ids[slot_no]] - iterate)
        applied = iterate - stiffness * laplace
        iterate = iterate + step_size * (modal_rhs - applied) / diagonal
    new_height = jnp.dot(from_modes, iterate, precision=lax.Precision.HIGHEST, preferred_element_type=jnp.float32)
    return new_winds, new_height
```

```python
import functools
import math

import jax
import jax.numpy as jnp
from jax import lax
from jax.experimental import pallas as pl
from jax.experimental.pallas import tpu as pltpu
from jax.sharding import PartitionSpec as P

CELLS = 2048
REACH = 512
NBR_REACH = 64
SWEEPS = 4
POINTS = 12
SIDES = 6
GROUPS = 8
ROWS = 12
SLAB = 16
LANES = 128
EDGE = 256
FIELD_EDGE = EDGE + REACH
WIDE = CELLS + 2 * EDGE
WIDE_BLOCKS = WIDE // LANES
CHUNK = CELLS // GROUPS
WINDOW = CHUNK + 2 * EDGE
TILES = 9
INNER_LO = FIELD_EDGE // LANES
INNER = (CELLS - 2 * REACH) // LANES
HALO_ROWS = 56
COUPLING = 0.5

f32 = jnp.float32
bf16 = jnp.bfloat16


def pack_fields(dst, dst_col, src, src_col, count):
    d = slice(dst_col, dst_col + count)
    s = slice(src_col, src_col + count)
    for field in range(3):
        dst[8 * field : 8 * field + 8, d] = src[field, 0:8, s]
        dst[24 + 4 * field : 28 + 4 * field, d] = src[field, 8:12, s]
    dst[36:40, d] = jnp.zeros((4, count), f32)


def halo_kernel(*refs):
    group, coef, *sources = refs[:9]
    head, tail, coef_row = refs[9:12]
    buffers, coef_here, sems = refs[12:26], refs[26], refs[27]
    copies = []
    for side, (field_col, col) in enumerate(((0, 0), (CELLS - FIELD_EDGE, CELLS - EDGE))):
        for n, source in enumerate(sources):
            cells = pl.ds(field_col, FIELD_EDGE) if n == 0 else pl.ds(col, EDGE)
            part = source.at[:, cells] if n > 2 else source.at[:, :, cells]
            copies.append(pltpu.make_async_copy(part, buffers[7 * side + n], sems.at[7 * side + n]))
    copies.append(pltpu.make_async_copy(coef, coef_here, sems.at[14]))
    for copy in copies:
        copy.start()
    for side, (out, col) in enumerate(((head, 0), (tail, CELLS - EDGE))):
        for copy in copies[7 * side : 7 * side + 7]:
            copy.wait()
        fields, index, weight, nbr, lap, ex, ey = buffers[7 * side : 7 * side + 7]
        pack_fields(out, 0, fields, 0, FIELD_EDGE)
        own = col + lax.broadcasted_iota(jnp.int32, (1, EDGE), 1)
        for p in range(POINTS):
            out[40 + p : 41 + p, 0:EDGE] = (index[p] - REACH - own).astype(f32)
            out[40 + p : 41 + p, EDGE : 2 * EDGE] = weight[p]
        away = (nbr[...] - NBR_REACH - own).astype(f32)
        out[52:56, 0:EDGE] = away[0:4]
        out[52:56, EDGE : 2 * EDGE] = lap[0:4]
        out[40:46, 2 * EDGE :] = ex[...]
        out[46:52, 2 * EDGE :] = ey[...]
        out[52:54, 2 * EDGE :] = away[4:6]
        out[54:56, 2 * EDGE :] = lap[4:6]
    copies[14].wait()
    lane = lax.broadcasted_iota(jnp.int32, (1, LANES), 1)
    row = jnp.zeros((1, LANES), f32)
    for k in range(ROWS):
        row = jnp.where(lane == group[0] * ROWS + k, coef_here[k], row)
    coef_row[...] = row


def stencil_block(x, col, away, weight, away_col):
    groups = 5
    acc = [jnp.zeros((8, LANES), f32) for _ in range(groups)]
    lane = lax.broadcasted_iota(jnp.int32, (1, LANES), 1)
    for p in range(POINTS):
        at = away[p, :, pl.ds(away_col, LANES)] + (lane + REACH)
        at = jnp.broadcast_to(at, (8, LANES))
        w = jnp.broadcast_to(weight[p, :, pl.ds(away_col, LANES)], (8, LANES))
        inside = at & (LANES - 1)
        tile = at >> 7
        picked = [None] * groups
        for t in range(TILES):
            mask = tile == t
            for g in range(groups):
                part = x[8 * g : 8 * g + 8, pl.ds(col + t * LANES, LANES)]
                part = jnp.take_along_axis(part, inside, axis=1, mode="promise_in_bounds")
                picked[g] = part if t == 0 else jnp.where(mask, part, picked[g])
        for g in range(groups):
            acc[g] = acc[g] + w * picked[g]
    return acc


def inner_kernel(fields, index, weight, coef_row, packed, upstream, away):
    pack_fields(packed, 0, fields, 0, CELLS)
    packed[36:37, 0:LANES] = coef_row[...]
    own = lax.broadcasted_iota(jnp.int32, (1, CELLS), 1)
    for p in range(POINTS):
        away[p] = index[p] - REACH - own

    def body(b, carry):
        col = pl.multiple_of(b * LANES, LANES)
        acc = stencil_block(packed, col, away, weight, pl.multiple_of(col + REACH, LANES))
        for g in range(5):
            upstream[8 * g : 8 * g + 8, pl.ds(col, LANES)] = acc[g]
        return carry

    lax.fori_loop(0, INNER, body, 0)


def outer_kernel(
    packed, inner, left, right, index, weight, nbr, ex, ey,
    winds, send, x, up, away, w_all, side, side_x, side_y, rs,
):
    x[:, 0:FIELD_EDGE] = left[0:40, :]
    x[:, FIELD_EDGE : FIELD_EDGE + CELLS] = packed[...]
    x[:, FIELD_EDGE + CELLS :] = right[0:40, :]
    own = lax.broadcasted_iota(jnp.int32, (1, CELLS), 1)
    mid = slice(EDGE, EDGE + CELLS)
    for halo, cells in ((left, slice(0, EDGE)), (right, slice(EDGE + CELLS, WIDE))):
        for p in range(POINTS):
            away[p, :, cells] = halo[40 + p : 41 + p, 0:EDGE].astype(jnp.int32)
            w_all[p, :, cells] = halo[40 + p : 41 + p, EDGE : 2 * EDGE]
        side[0:4, cells] = halo[52:56, 0:EDGE].astype(jnp.int32)
        side[4:6, cells] = halo[52:54, 2 * EDGE :].astype(jnp.int32)
        side_x[:, cells] = halo[40:46, 2 * EDGE :]
        side_y[:, cells] = halo[46:52, 2 * EDGE :]
    for p in range(POINTS):
        away[p, :, mid] = index[p] - REACH - own
        w_all[p, :, mid] = weight[p]
    side[:, mid] = nbr[...] - NBR_REACH - own
    side_x[:, mid] = ex[...]
    side_y[:, mid] = ey[...]

    up[:, 0:LANES] = jnp.zeros((40, LANES), f32)
    up[:, LANES + WIDE :] = jnp.zeros((40, LANES), f32)
    first = LANES * (1 + INNER_LO)
    up[:, first : first + INNER * LANES] = inner[...]

    def stencil(i, carry):
        b = jnp.where(i < INNER_LO, i, i + INNER)
        col = pl.multiple_of(b * LANES, LANES)
        acc = stencil_block(x, col, away, w_all, col)
        for g in range(5):
            up[8 * g : 8 * g + 8, pl.ds(col + LANES, LANES)] = acc[g]
        return carry

    lax.fori_loop(0, WIDE_BLOCKS - INNER, stencil, 0)

    for field in range(2):
        cells = slice(LANES + EDGE, LANES + EDGE + CELLS)
        winds[field, 0:8, :] = up[8 * field : 8 * field + 8, cells]
        winds[field, 8:12, :] = up[24 + 4 * field : 28 + 4 * field, cells]

    lane = lax.broadcasted_iota(jnp.int32, (1, LANES), 1)
    upper = lax.broadcasted_iota(jnp.int32, (8, LANES), 0) < 4

    def divergence(b, carry):
        col = pl.multiple_of(b * LANES, LANES)
        rows = (0, 8, 24)
        here = [up[r : r + 8, pl.ds(col + LANES, LANES)] for r in rows]
        acc = [jnp.zeros((8, LANES), f32) for _ in rows]
        for k in range(SIDES):
            at = jnp.broadcast_to(side[k : k + 1, pl.ds(col, LANES)] + (lane + LANES), (8, LANES))
            inside = at & (LANES - 1)
            tile = at >> 7
            wx = jnp.broadcast_to(side_x[k : k + 1, pl.ds(col, LANES)], (8, LANES))
            wy = jnp.broadcast_to(side_y[k : k + 1, pl.ds(col, LANES)], (8, LANES))
            weights = (wx, wy, jnp.where(upper, wx, wy))
            for g, r in enumerate(rows):
                picked = None
                for t in range(3):
                    part = up[r : r + 8, pl.ds(col + t * LANES, LANES)]
                    part = jnp.take_along_axis(part, inside, axis=1, mode="promise_in_bounds")
                    picked = part if t == 0 else jnp.where(tile == t, part, picked)
                acc[g] = acc[g] + weights[g] * (picked - here[g])
        h0 = up[16:24, pl.ds(col + LANES, LANES)]
        h1 = up[32:36, pl.ds(col + LANES, LANES)]
        rs[0:8, pl.ds(col, LANES)] = h0 - COUPLING * (acc[0] + acc[1])
        rs[8:12, pl.ds(col, LANES)] = h1 - COUPLING * (acc[2][0:4] + acc[2][4:8])
        return carry

    lax.fori_loop(0, WIDE_BLOCKS, divergence, 0)

    rs[12:16, :] = jnp.zeros((4, WIDE), f32)
    for j in range(GROUPS):
        send[j] = rs[:, j * CHUNK : j * CHUNK + WINDOW]
        send[j, 12:13, 0:LANES] = packed[36:37, 0:LANES]


def split(v):
    high = v.astype(bf16)
    return high, (v - high.astype(f32)).astype(bf16)


def dot3(a, b):
    ah, al = a
    bh, bl = b
    dot = functools.partial(jnp.dot, preferred_element_type=f32)
    return dot(ah, bh) + (dot(al, bh) + dot(ah, bl))


def band_kernel(group, left, right, nbr, lap, high, low, total, side, side_w):
    own = lax.broadcasted_iota(jnp.int32, (1, CELLS), 1)
    mid = slice(EDGE, EDGE + CELLS)
    for halo, cells in ((left, slice(0, EDGE)), (right, slice(EDGE + CELLS, WIDE))):
        side[0:4, cells] = halo[52:56, 0:EDGE].astype(jnp.int32)
        side[4:6, cells] = halo[52:54, 2 * EDGE :].astype(jnp.int32)
        side_w[0:4, cells] = halo[52:56, EDGE : 2 * EDGE]
        side_w[4:6, cells] = halo[54:56, 2 * EDGE :]
    side[:, mid] = nbr[...] - NBR_REACH - own
    side_w[:, mid] = lap[...]
    start = pl.multiple_of(group[0] * CHUNK, LANES)
    total[...] = jnp.sum(side_w[:, pl.ds(start, WINDOW)], axis=0, keepdims=True)
    lane = lax.broadcasted_iota(jnp.int32, (1, LANES), 1)
    slot = lax.broadcasted_iota(jnp.int32, (3 * LANES, LANES), 0)
    for b in range(4):
        cells = pl.ds(pl.multiple_of(start + (b + 1) * LANES, LANES), LANES)
        matrix = jnp.zeros((3 * LANES, LANES), f32)
        for k in range(SIDES):
            at = side[k : k + 1, cells] + (lane + LANES)
            matrix = matrix + jnp.where(slot == at, side_w[k : k + 1, cells], 0.0)
        high[b], low[b] = split(matrix)


def solve_kernel(got, high, low, total, to_modes, from_modes, out):
    levels = got[...].reshape(GROUPS * SLAB, WINDOW)
    modes = GROUPS * ROWS
    coef_row = got[0, 12:13, 0:LANES]
    for j in range(1, GROUPS):
        coef_row = coef_row + got[j, 12:13, 0:LANES]
    eye = lax.broadcasted_iota(jnp.int32, (modes, LANES), 0) == lax.broadcasted_iota(
        jnp.int32, (modes, LANES), 1
    )
    coef = jnp.sum(jnp.where(eye, coef_row, 0.0), axis=1, keepdims=True)
    rhs = dot3(split(to_modes[...]), split(levels))
    inverse = 1.0 / (1.0 + coef * total[...])
    rhs = rhs * inverse
    scaled = coef * inverse
    radius = 6.0 * coef / (1.0 + 6.0 * coef)
    steps = [
        1.0 / (1.0 + radius * math.cos(math.pi * (2 * s + 1) / (2.0 * SWEEPS)))
        for s in range(SWEEPS)
    ]
    cols = [slice(b * LANES, (b + 1) * LANES) for b in range(6)]
    iterate = [steps[0] * rhs[:, c] for c in cols]
    for sweep, blocks in ((1, (1, 2, 3, 4)), (2, (1, 2, 3, 4)), (3, (2, 3))):
        parts = [split(v) for v in iterate]
        step = steps[sweep]
        fresh = list(iterate)
        for b in blocks:
            near = [jnp.concatenate([parts[b + o][i] for o in (-1, 0, 1)], axis=1) for i in (0, 1)]
            moved = dot3(near, (high[b - 1], low[b - 1]))
            fresh[b] = (1.0 - step) * iterate[b] + step * (
                rhs[:, cols[b]] + scaled[:, cols[b]] * moved
            )
        iterate = fresh
    solved = jnp.concatenate([iterate[2], iterate[3]], axis=1)
    height = dot3(split(from_modes[...]), split(solved))
    out[...] = height.reshape(GROUPS, SLAB, CHUNK)


def place_kernel(got, out):
    for j in range(GROUPS):
        out[:, j * CHUNK : (j + 1) * CHUNK] = got[j, 0:ROWS, :]


def call(kernel, outs, scratch=(), name=None, smem=0, n_in=0, space=pltpu.VMEM, vmem=32):
    in_specs = [pl.BlockSpec(memory_space=pltpu.SMEM)] * smem + [
        pl.BlockSpec(memory_space=space)
    ] * (n_in - smem)
    shapes = [jax.ShapeDtypeStruct(s, d) for s, d in outs]
    specs = [pl.BlockSpec(memory_space=pltpu.VMEM)] * len(outs)
    if len(outs) == 1:
        shapes, specs = shapes[0], specs[0]
    return pl.pallas_call(
        kernel,
        out_shape=shapes,
        in_specs=in_specs,
        out_specs=specs,
        scratch_shapes=list(scratch),
        name=name,
        compiler_params=pltpu.CompilerParams(vmem_limit_bytes=int(vmem * 1024 * 1024)),
    )


def per_device(
    fields,
    stencil_index,
    stencil_weight,
    neighbours,
    lap_weight,
    edge_x,
    edge_y,
    to_modes,
    from_modes,
    helm_coef,
):
    patches = lax.axis_size("patch")
    group = lax.axis_index("lev")
    halo = ((HALO_ROWS, FIELD_EDGE), f32)
    buffers = [
        pltpu.VMEM((3, ROWS, FIELD_EDGE), f32),
        pltpu.VMEM((POINTS, 1, EDGE), jnp.int32),
        pltpu.VMEM((POINTS, 1, EDGE), f32),
        pltpu.VMEM((SIDES, EDGE), jnp.int32),
    ] + [pltpu.VMEM((SIDES, EDGE), f32)] * 3
    head, tail, coef_row = call(
        halo_kernel,
        [halo, halo, ((1, LANES), f32)],
        buffers * 2 + [pltpu.SMEM((ROWS,), f32), pltpu.SemaphoreType.DMA((15,))],
        name="halo",
        smem=1,
        n_in=9,
        space=pltpu.HBM,
        vmem=62,
    )(
        group[None], helm_coef, fields, stencil_index, stencil_weight, neighbours, lap_weight,
        edge_x, edge_y,
    )
    left = lax.ppermute(tail, "patch", [(i, (i + 1) % patches) for i in range(patches)])
    right = lax.ppermute(head, "patch", [((i + 1) % patches, i) for i in range(patches)])
    packed, inner = call(
        inner_kernel,
        [((40, CELLS), f32), ((40, INNER * LANES), f32)],
        [pltpu.VMEM((POINTS, 1, CELLS), jnp.int32)],
        name="inner",
        n_in=4,
    )(fields, stencil_index, stencil_weight, coef_row)
    new_winds, send = call(
        outer_kernel,
        [((2, ROWS, CELLS), f32), ((GROUPS, SLAB, WINDOW), f32)],
        [
            pltpu.VMEM((40, CELLS + 2 * FIELD_EDGE), f32),
            pltpu.VMEM((40, WIDE + 2 * LANES), f32),
            pltpu.VMEM((POINTS, 1, WIDE), jnp.int32),
            pltpu.VMEM((POINTS, 1, WIDE), f32),
            pltpu.VMEM((SIDES, WIDE), jnp.int32),
            pltpu.VMEM((SIDES, WIDE), f32),
            pltpu.VMEM((SIDES, WIDE), f32),
            pltpu.VMEM((SLAB, WIDE), f32),
        ],
        name="outer",
        n_in=9,
    )(
        packed, inner, left, right, stencil_index, stencil_weight,
        neighbours, edge_x, edge_y,
    )
    high, low, total = call(
        band_kernel,
        [((4, 3 * LANES, LANES), bf16), ((4, 3 * LANES, LANES), bf16), ((1, WINDOW), f32)],
        [pltpu.VMEM((SIDES, WIDE), jnp.int32), pltpu.VMEM((SIDES, WIDE), f32)],
        name="band",
        smem=1,
        n_in=5,
    )(group[None], left, right, neighbours, lap_weight)
    got = lax.all_to_all(send, "lev", split_axis=0, concat_axis=0, tiled=True)
    pad = ((0, 0), (0, 0), (0, SLAB - ROWS))
    modes = GROUPS * ROWS
    to_wide = jnp.pad(to_modes.reshape(modes, GROUPS, ROWS), pad).reshape(modes, GROUPS * SLAB)
    from_wide = jnp.pad(
        from_modes.reshape(GROUPS, ROWS, modes), ((0, 0), (0, SLAB - ROWS), (0, 0))
    ).reshape(GROUPS * SLAB, modes)
    heights = call(solve_kernel, [((GROUPS, SLAB, CHUNK), f32)], name="solve", n_in=6)(
        got, high, low, total, to_wide, from_wide
    )
    heights = lax.all_to_all(heights, "lev", split_axis=0, concat_axis=0, tiled=True)
    new_height = call(place_kernel, [((ROWS, CELLS), f32)], name="place", n_in=1)(heights)
    return new_winds, new_height


def solution(mesh):
    in_specs = (
        P(None, "lev", "patch"),
        P(None, "lev", "patch"),
        P(None, "lev", "patch"),
        P(None, "patch"),
        P(None, "patch"),
        P(None, "patch"),
        P(None, "patch"),
        P(),
        P(),
        P("lev"),
    )
    out_specs = (P(None, "lev", "patch"), P("lev", "patch"))
    return jax.shard_map(
        per_device, mesh=mesh, in_specs=in_specs, out_specs=out_specs, check_vma=False
    )
```

```python
import functools
import math

import jax
import jax.numpy as jnp
from jax import lax
from jax.experimental import pallas as pl
from jax.experimental.pallas import tpu as pltpu
from jax.sharding import PartitionSpec as P

CELLS = 2048
REACH = 512
NBR_REACH = 64
SWEEPS = 4
POINTS = 12
SIDES = 6
GROUPS = 8
ROWS = 12
LANES = 128
EDGE = 256
FIELD_EDGE = EDGE + REACH
WIDE = CELLS + 2 * EDGE
WIDE_BLOCKS = WIDE // LANES
CHUNK = CELLS // GROUPS
WINDOW = CHUNK + 2 * EDGE
TILES = 9
INNER_LO = FIELD_EDGE // LANES
INNER = (CELLS - 2 * REACH) // LANES
MATRIX = 8
HALF = WINDOW // 2
HALO_ROWS = 56
COUPLING = 0.5

f32 = jnp.float32
bf16 = jnp.bfloat16


def pack_fields(dst, dst_col, src, src_col, count):
    d = slice(dst_col, dst_col + count)
    s = slice(src_col, src_col + count)
    for field in range(3):
        dst[8 * field : 8 * field + 8, d] = src[field, 0:8, s]
        dst[24 + 4 * field : 28 + 4 * field, d] = src[field, 8:12, s]
    dst[36:40, d] = jnp.zeros((4, count), f32)


def halo_kernel(*refs):
    group, coef, *sources = refs[:9]
    head, tail, coef_row = refs[9:12]
    buffers, coef_here, sems = refs[12:26], refs[26], refs[27]
    copies = []
    for side, (field_col, col) in enumerate(((0, 0), (CELLS - FIELD_EDGE, CELLS - EDGE))):
        for n, source in enumerate(sources):
            cells = pl.ds(field_col, FIELD_EDGE) if n == 0 else pl.ds(col, EDGE)
            part = source.at[:, cells] if n > 2 else source.at[:, :, cells]
            copies.append(pltpu.make_async_copy(part, buffers[7 * side + n], sems.at[7 * side + n]))
    copies.append(pltpu.make_async_copy(coef, coef_here, sems.at[14]))
    for copy in copies:
        copy.start()
    for side, (out, col) in enumerate(((head, 0), (tail, CELLS - EDGE))):
        for copy in copies[7 * side : 7 * side + 7]:
            copy.wait()
        fields, index, weight, nbr, lap, ex, ey = buffers[7 * side : 7 * side + 7]
        pack_fields(out, 0, fields, 0, FIELD_EDGE)
        own = col + lax.broadcasted_iota(jnp.int32, (1, EDGE), 1)
        for p in range(POINTS):
            out[40 + p : 41 + p, 0:EDGE] = (index[p] - REACH - own).astype(f32)
            out[40 + p : 41 + p, EDGE : 2 * EDGE] = weight[p]
        away = (nbr[...] - NBR_REACH - own).astype(f32)
        out[52:56, 0:EDGE] = away[0:4]
        out[52:56, EDGE : 2 * EDGE] = lap[0:4]
        out[40:46, 2 * EDGE :] = ex[...]
        out[46:52, 2 * EDGE :] = ey[...]
        out[52:54, 2 * EDGE :] = away[4:6]
        out[54:56, 2 * EDGE :] = lap[4:6]
    copies[14].wait()
    lane = lax.broadcasted_iota(jnp.int32, (1, LANES), 1)
    row = jnp.zeros((1, LANES), f32)
    for k in range(ROWS):
        row = jnp.where(lane == group[0] * ROWS + k, coef_here[k], row)
    coef_row[...] = row


def split(v):
    high = v.astype(bf16)
    return high, (v - high.astype(f32)).astype(bf16)


def split_tiles(dst, first, src, src_col, count):
    for t in range(count):
        high, low = split(src[0:40, src_col + t * LANES : src_col + (t + 1) * LANES])
        dst[first + t, :, 0:LANES] = high
        dst[first + t, :, LANES:] = low


def stencil_block(x, slabs, first, col, away, weight, away_col):
    groups = 5
    acc = [jnp.zeros((8, LANES), f32) for _ in range(groups)]
    lane = lax.broadcasted_iota(jnp.int32, (1, LANES), 1)
    slot = lax.broadcasted_iota(jnp.int32, (LANES, LANES), 0).astype(bf16)
    ones = jnp.ones((LANES, LANES), bf16)
    near = slabs[pl.ds(first, TILES)].reshape(TILES * 8 * groups, 2 * LANES)

    def locate(p):
        at = away[p, :, pl.ds(away_col, LANES)] + (lane + REACH)
        w = jnp.broadcast_to(weight[p, :, pl.ds(away_col, LANES)], (8, LANES))
        return at & (LANES - 1), jnp.broadcast_to(at >> 7, (8, LANES)), w

    def add(part, tile, w):
        picked = [None] * groups
        for t in range(TILES):
            mask = tile == t
            for g in range(groups):
                picked[g] = part(t, g) if t == 0 else jnp.where(mask, part(t, g), picked[g])
        for g in range(groups):
            acc[g] = acc[g] + w * picked[g]

    def one_hot(inside):
        at = jnp.broadcast_to(inside.astype(f32), (LANES, LANES)).astype(bf16)
        return jnp.where(slot == at, ones, jnp.zeros_like(ones))

    def gathered(p):
        inside, tile, w = locate(p)
        inside = jnp.broadcast_to(inside, (8, LANES))

        def part(t, g):
            rows = x[8 * g : 8 * g + 8, pl.ds(col + t * LANES, LANES)]
            return jnp.take_along_axis(rows, inside, axis=1, mode="promise_in_bounds")

        add(part, tile, w)

    plain = list(range(MATRIX, POINTS))
    for pair in range(0, MATRIX, 2):
        points = [locate(p) for p in (pair, pair + 1)]
        hot = jnp.concatenate([one_hot(inside) for inside, _, _ in points], axis=1)
        rows = jnp.dot(near, jnp.concatenate([hot, hot], axis=0), preferred_element_type=f32)
        if plain:
            gathered(plain.pop(0))
        for i, (_, tile, w) in enumerate(points):
            c = slice(i * LANES, (i + 1) * LANES)
            add(lambda t, g: rows[40 * t + 8 * g : 40 * t + 8 * g + 8, c], tile, w)
    for p in plain:
        gathered(p)
    return acc


def right_side_block(up, up_col, side, side_x, side_y, col):
    lane = lax.broadcasted_iota(jnp.int32, (1, LANES), 1)
    upper = lax.broadcasted_iota(jnp.int32, (8, LANES), 0) < 4
    rows = (0, 8, 24)
    here = [up[r : r + 8, pl.ds(up_col + LANES, LANES)] for r in rows]
    acc = [jnp.zeros((8, LANES), f32) for _ in rows]
    for k in range(SIDES):
        at = jnp.broadcast_to(side[k : k + 1, pl.ds(col, LANES)] + (lane + LANES), (8, LANES))
        inside = at & (LANES - 1)
        tile = at >> 7
        wx = jnp.broadcast_to(side_x[k : k + 1, pl.ds(col, LANES)], (8, LANES))
        wy = jnp.broadcast_to(side_y[k : k + 1, pl.ds(col, LANES)], (8, LANES))
        weights = (wx, wy, jnp.where(upper, wx, wy))
        for g, r in enumerate(rows):
            picked = None
            for t in range(3):
                part = up[r : r + 8, pl.ds(up_col + t * LANES, LANES)]
                part = jnp.take_along_axis(part, inside, axis=1, mode="promise_in_bounds")
                picked = part if t == 0 else jnp.where(tile == t, part, picked)
            acc[g] = acc[g] + weights[g] * (picked - here[g])
    top = up[16:24, pl.ds(up_col + LANES, LANES)] - COUPLING * (acc[0] + acc[1])
    rest = up[32:36, pl.ds(up_col + LANES, LANES)] - COUPLING * (acc[2][0:4] + acc[2][4:8])
    return top, rest


def inner_kernel(
    fields, index, weight, nbr, ex, ey, coef_row,
    packed, slabs, upstream, right, away, side,
):
    pack_fields(packed, 0, fields, 0, CELLS)
    packed[36:37, 0:LANES] = coef_row[...]
    split_tiles(slabs, 0, packed, 0, CELLS // LANES)
    own = lax.broadcasted_iota(jnp.int32, (1, CELLS), 1)
    for p in range(POINTS):
        away[p] = index[p] - REACH - own
    side[...] = nbr[...] - NBR_REACH - own

    def stencil(b, carry):
        col = pl.multiple_of(b * LANES, LANES)
        acc = stencil_block(
            packed, slabs, b, col, away, weight, pl.multiple_of(col + REACH, LANES)
        )
        for g in range(5):
            upstream[8 * g : 8 * g + 8, pl.ds(col, LANES)] = acc[g]
        return carry

    lax.fori_loop(0, INNER, stencil, 0, unroll=4)

    def finish(b, carry):
        col = pl.multiple_of(b * LANES, LANES)
        top, rest = right_side_block(
            upstream, col, side, ex, ey, pl.multiple_of(col + REACH + LANES, LANES)
        )
        right[0:8, pl.ds(col, LANES)] = top
        right[8:12, pl.ds(col, LANES)] = rest
        return carry

    lax.fori_loop(0, INNER - 2, finish, 0, unroll=2)


def outer_kernel(
    packed, own_slabs, inner, inner_right, left, right, index, weight, nbr, ex, ey,
    winds, send, x, slabs, up, away, w_all, side, side_x, side_y, rs, rest_rs,
):
    halo_tiles = FIELD_EDGE // LANES
    x[:, 0:FIELD_EDGE] = left[0:40, :]
    x[:, FIELD_EDGE : FIELD_EDGE + CELLS] = packed[...]
    x[:, FIELD_EDGE + CELLS :] = right[0:40, :]
    split_tiles(slabs, 0, left, 0, halo_tiles)
    slabs[halo_tiles : halo_tiles + CELLS // LANES] = own_slabs[...]
    split_tiles(slabs, halo_tiles + CELLS // LANES, right, 0, halo_tiles)
    own = lax.broadcasted_iota(jnp.int32, (1, CELLS), 1)
    mid = slice(EDGE, EDGE + CELLS)
    for halo, cells in ((left, slice(0, EDGE)), (right, slice(EDGE + CELLS, WIDE))):
        for p in range(POINTS):
            away[p, :, cells] = halo[40 + p : 41 + p, 0:EDGE].astype(jnp.int32)
            w_all[p, :, cells] = halo[40 + p : 41 + p, EDGE : 2 * EDGE]
        side[0:4, cells] = halo[52:56, 0:EDGE].astype(jnp.int32)
        side[4:6, cells] = halo[52:54, 2 * EDGE :].astype(jnp.int32)
        side_x[:, cells] = halo[40:46, 2 * EDGE :]
        side_y[:, cells] = halo[46:52, 2 * EDGE :]
    for start in (0, CELLS - REACH):
        there = start + lax.broadcasted_iota(jnp.int32, (1, REACH), 1)
        cells = slice(EDGE + start, EDGE + start + REACH)
        for p in range(POINTS):
            away[p, :, cells] = index[p, :, start : start + REACH] - REACH - there
            w_all[p, :, cells] = weight[p, :, start : start + REACH]
    side[:, mid] = nbr[...] - NBR_REACH - own
    side_x[:, mid] = ex[...]
    side_y[:, mid] = ey[...]

    up[:, 0:LANES] = jnp.zeros((40, LANES), f32)
    up[:, LANES + WIDE :] = jnp.zeros((40, LANES), f32)
    first = LANES * (1 + INNER_LO)
    up[:, first : first + INNER * LANES] = inner[...]

    def stencil(i, carry):
        for b in (i, i + INNER_LO + INNER):
            col = pl.multiple_of(b * LANES, LANES)
            acc = stencil_block(x, slabs, b, col, away, w_all, col)
            for g in range(5):
                up[8 * g : 8 * g + 8, pl.ds(col + LANES, LANES)] = acc[g]
        return carry

    lax.fori_loop(0, INNER_LO, stencil, 0, unroll=3)

    for field in range(2):
        cells = slice(LANES + EDGE, LANES + EDGE + CELLS)
        winds[field, 0:8, :] = up[8 * field : 8 * field + 8, cells]
        winds[field, 8:12, :] = up[24 + 4 * field : 28 + 4 * field, cells]

    first = (INNER_LO + 1) * LANES
    last = first + (INNER - 2) * LANES
    rs[:, first:last] = inner_right[0:8, :]
    rest_rs[0:4, HALF + first : HALF + last] = inner_right[8:12, :]
    rest_rs[4:8, first:last] = inner_right[8:12, :]

    def finish(i, carry):
        for b in (i, i + INNER_LO + INNER - 1):
            col = pl.multiple_of(b * LANES, LANES)
            top, rest = right_side_block(up, col, side, side_x, side_y, col)
            rs[:, pl.ds(col, LANES)] = top
            rest_rs[0:4, pl.ds(col + HALF, LANES)] = rest
            rest_rs[4:8, pl.ds(col, LANES)] = rest
        return carry

    lax.fori_loop(0, INNER_LO + 1, finish, 0)

    lane = lax.broadcasted_iota(jnp.int32, (1, LANES), 1)
    coef = packed[36:37, 0:LANES]
    for j in range(GROUPS):
        col = j * CHUNK
        send[j, :, 0:WINDOW] = rs[:, col : col + WINDOW]
        send[j, :, WINDOW:] = rest_rs[:, HALF + col : 2 * HALF + col]
        send[j, 0:1, 0:LANES] = jnp.where(lane < NBR_REACH, coef, rs[0:1, col : col + LANES])
        col = col + WINDOW - LANES
        send[j, 0:1, WINDOW - LANES : WINDOW] = jnp.where(
            lane < NBR_REACH, rs[0:1, col : col + LANES], coef
        )


def dot3(a, b):
    ah, al = a
    bh, bl = b
    dot = functools.partial(jnp.dot, preferred_element_type=f32)
    return dot(ah, bh) + (dot(al, bh) + dot(ah, bl))


def band_kernel(group, left, right, nbr, lap, high, low, total, side, side_w):
    own = lax.broadcasted_iota(jnp.int32, (1, CELLS), 1)
    mid = slice(EDGE, EDGE + CELLS)
    for halo, cells in ((left, slice(0, EDGE)), (right, slice(EDGE + CELLS, WIDE))):
        side[0:4, cells] = halo[52:56, 0:EDGE].astype(jnp.int32)
        side[4:6, cells] = halo[52:54, 2 * EDGE :].astype(jnp.int32)
        side_w[0:4, cells] = halo[52:56, EDGE : 2 * EDGE]
        side_w[4:6, cells] = halo[54:56, 2 * EDGE :]
    side[:, mid] = nbr[...] - NBR_REACH - own
    side_w[:, mid] = lap[...]
    start = pl.multiple_of(group[0] * CHUNK, LANES)
    total[...] = jnp.sum(side_w[:, pl.ds(start, WINDOW)], axis=0, keepdims=True)
    lane = lax.broadcasted_iota(jnp.int32, (1, LANES), 1)
    slot = lax.broadcasted_iota(jnp.int32, (3 * LANES, LANES), 0)
    for b in range(4):
        cells = pl.ds(pl.multiple_of(start + (b + 1) * LANES, LANES), LANES)
        matrix = jnp.zeros((3 * LANES, LANES), f32)
        for k in range(SIDES):
            at = side[k : k + 1, cells] + (lane + LANES)
            matrix = matrix + jnp.where(slot == at, side_w[k : k + 1, cells], 0.0)
        high[b], low[b] = split(matrix)


def solve_kernel(got, high, low, total, to_first, to_second, from_first, from_second, out):
    modes = GROUPS * ROWS
    lane = lax.broadcasted_iota(jnp.int32, (1, LANES), 1)
    left = got[:, 0, 0:LANES]
    right = got[:, 0, WINDOW - LANES : WINDOW]
    coef_row = jnp.sum(jnp.where(lane < NBR_REACH, left, right), axis=0, keepdims=True)
    eye = lax.broadcasted_iota(jnp.int32, (modes, LANES), 0) == lax.broadcasted_iota(
        jnp.int32, (modes, LANES), 1
    )
    coef = jnp.sum(jnp.where(eye, coef_row, 0.0), axis=1, keepdims=True)
    rows = GROUPS * 8
    main = split(got[:, :, 0:WINDOW].reshape(rows, WINDOW))
    rest = split(got[:, :, WINDOW:].reshape(rows, HALF))
    halves = []
    for matrix, cols in ((to_first, slice(0, HALF)), (to_second, slice(HALF, WINDOW))):
        levels = tuple(jnp.concatenate([m[:, cols], r], axis=0) for m, r in zip(main, rest))
        halves.append(dot3(split(matrix[...]), levels))
    rhs = jnp.concatenate(halves, axis=1)
    inverse = 1.0 / (1.0 + coef * total[...])
    rhs = rhs * inverse
    scaled = coef * inverse
    radius = 6.0 * coef / (1.0 + 6.0 * coef)
    steps = [
        1.0 / (1.0 + radius * math.cos(math.pi * (2 * s + 1) / (2.0 * SWEEPS)))
        for s in range(SWEEPS)
    ]
    cols = [slice(b * LANES, (b + 1) * LANES) for b in range(6)]
    iterate = [steps[0] * rhs[:, c] for c in cols]
    for sweep, blocks in ((1, (1, 2, 3, 4)), (2, (1, 2, 3, 4)), (3, (2, 3))):
        parts = [jnp.concatenate(split(v), axis=0) for v in iterate]
        step = steps[sweep]
        fresh = list(iterate)
        for b in blocks:
            near = jnp.concatenate(parts[b - 1 : b + 2], axis=1)
            both = jnp.concatenate([high[b - 1], low[b - 1]], axis=1)
            four = jnp.dot(near, both, preferred_element_type=f32)
            moved = four[:modes, :LANES] + (
                four[modes:, :LANES] + four[:modes, LANES:] + four[modes:, LANES:]
            )
            fresh[b] = (1.0 - step) * iterate[b] + step * (
                rhs[:, cols[b]] + scaled[:, cols[b]] * moved
            )
        iterate = fresh
    first = dot3(split(from_first[...]), split(iterate[2]))
    second = dot3(split(from_second[...]), split(iterate[3]))
    shape = (GROUPS, 8, LANES)
    out[:, :, 0:LANES] = first[:rows].reshape(shape)
    out[:, :, LANES:CHUNK] = second[:rows].reshape(shape)
    out[:, :, CHUNK:] = (first[rows:] + second[rows:]).reshape(shape)


def place_kernel(got, out):
    for j in range(GROUPS):
        col = j * CHUNK
        out[0:8, col : col + CHUNK] = got[j, :, 0:CHUNK]
        out[8:12, col : col + LANES] = got[j, 0:4, CHUNK:]
        out[8:12, col + LANES : col + CHUNK] = got[j, 4:8, CHUNK:]


def slab_order(matrix):
    groups = matrix.reshape(GROUPS, ROWS, -1)
    main = groups[:, 0:8].reshape(GROUPS * 8, -1)
    pads = (((0, 0), (0, 4), (0, 0)), ((0, 0), (4, 0), (0, 0)))
    return [
        jnp.concatenate([main, jnp.pad(groups[:, 8:12], pad).reshape(GROUPS * 8, -1)], axis=0)
        for pad in pads
    ]


def call(kernel, outs, scratch=(), name=None, smem=0, n_in=0, space=pltpu.VMEM, vmem=32):
    in_specs = [pl.BlockSpec(memory_space=pltpu.SMEM)] * smem + [
        pl.BlockSpec(memory_space=space)
    ] * (n_in - smem)
    shapes = [jax.ShapeDtypeStruct(s, d) for s, d in outs]
    specs = [pl.BlockSpec(memory_space=pltpu.VMEM)] * len(outs)
    if len(outs) == 1:
        shapes, specs = shapes[0], specs[0]
    return pl.pallas_call(
        kernel,
        out_shape=shapes,
        in_specs=in_specs,
        out_specs=specs,
        scratch_shapes=list(scratch),
        name=name,
        compiler_params=pltpu.CompilerParams(vmem_limit_bytes=int(vmem * 1024 * 1024)),
    )


def per_device(
    fields,
    stencil_index,
    stencil_weight,
    neighbours,
    lap_weight,
    edge_x,
    edge_y,
    to_modes,
    from_modes,
    helm_coef,
):
    patches = lax.axis_size("patch")
    group = lax.axis_index("lev")
    halo = ((HALO_ROWS, FIELD_EDGE), f32)
    buffers = [
        pltpu.VMEM((3, ROWS, FIELD_EDGE), f32),
        pltpu.VMEM((POINTS, 1, EDGE), jnp.int32),
        pltpu.VMEM((POINTS, 1, EDGE), f32),
        pltpu.VMEM((SIDES, EDGE), jnp.int32),
    ] + [pltpu.VMEM((SIDES, EDGE), f32)] * 3
    head, tail, coef_row = call(
        halo_kernel,
        [halo, halo, ((1, LANES), f32)],
        buffers * 2 + [pltpu.SMEM((ROWS,), f32), pltpu.SemaphoreType.DMA((15,))],
        name="halo",
        smem=1,
        n_in=9,
        space=pltpu.HBM,
        vmem=62,
    )(
        group[None], helm_coef, fields, stencil_index, stencil_weight, neighbours, lap_weight,
        edge_x, edge_y,
    )
    left = lax.ppermute(tail, "patch", [(i, (i + 1) % patches) for i in range(patches)])
    right = lax.ppermute(head, "patch", [((i + 1) % patches, i) for i in range(patches)])
    tiles = CELLS // LANES
    packed, slabs, inner, inner_right = call(
        inner_kernel,
        [
            ((40, CELLS), f32),
            ((tiles, 40, 2 * LANES), bf16),
            ((40, INNER * LANES), f32),
            ((ROWS, (INNER - 2) * LANES), f32),
        ],
        [pltpu.VMEM((POINTS, 1, CELLS), jnp.int32), pltpu.VMEM((SIDES, CELLS), jnp.int32)],
        name="inner",
        n_in=7,
    )(fields, stencil_index, stencil_weight, neighbours, edge_x, edge_y, coef_row)
    new_winds, send = call(
        outer_kernel,
        [((2, ROWS, CELLS), f32), ((GROUPS, 8, WINDOW + HALF), f32)],
        [
            pltpu.VMEM((40, CELLS + 2 * FIELD_EDGE), f32),
            pltpu.VMEM((tiles + 2 * FIELD_EDGE // LANES, 40, 2 * LANES), bf16),
            pltpu.VMEM((40, WIDE + 2 * LANES), f32),
            pltpu.VMEM((POINTS, 1, WIDE), jnp.int32),
            pltpu.VMEM((POINTS, 1, WIDE), f32),
            pltpu.VMEM((SIDES, WIDE), jnp.int32),
            pltpu.VMEM((SIDES, WIDE), f32),
            pltpu.VMEM((SIDES, WIDE), f32),
            pltpu.VMEM((8, WIDE), f32),
            pltpu.VMEM((8, WIDE + HALF), f32),
        ],
        name="outer",
        n_in=11,
    )(
        packed, slabs, inner, inner_right, left, right, stencil_index, stencil_weight,
        neighbours, edge_x, edge_y,
    )
    high, low, total = call(
        band_kernel,
        [((4, 3 * LANES, LANES), bf16), ((4, 3 * LANES, LANES), bf16), ((1, WINDOW), f32)],
        [pltpu.VMEM((SIDES, WIDE), jnp.int32), pltpu.VMEM((SIDES, WIDE), f32)],
        name="band",
        smem=1,
        n_in=5,
    )(group[None], left, right, neighbours, lap_weight)
    got = lax.all_to_all(send, "lev", split_axis=0, concat_axis=0, tiled=True)
    to_slabs = [m.T for m in slab_order(to_modes.T)]
    heights = call(solve_kernel, [((GROUPS, 8, CHUNK + LANES), f32)], name="solve", n_in=8)(
        got, high, low, total, *to_slabs, *slab_order(from_modes)
    )
    heights = lax.all_to_all(heights, "lev", split_axis=0, concat_axis=0, tiled=True)
    new_height = call(place_kernel, [((ROWS, CELLS), f32)], name="place", n_in=1)(heights)
    return new_winds, new_height


def solution(mesh):
    in_specs = (
        P(None, "lev", "patch"),
        P(None, "lev", "patch"),
        P(None, "lev", "patch"),
        P(None, "patch"),
        P(None, "patch"),
        P(None, "patch"),
        P(None, "patch"),
        P(),
        P(),
        P("lev"),
    )
    out_specs = (P(None, "lev", "patch"), P("lev", "patch"))
    return jax.shard_map(
        per_device, mesh=mesh, in_specs=in_specs, out_specs=out_specs, check_vma=False
    )
```

```python
import functools
import math

import jax
import jax.numpy as jnp
from jax import lax
from jax.experimental import pallas as pl
from jax.experimental.pallas import tpu as pltpu
from jax.sharding import PartitionSpec as P

CELLS = 2048
REACH = 512
NBR_REACH = 64
SWEEPS = 4
POINTS = 12
SIDES = 6
GROUPS = 8
ROWS = 12
LANES = 128
EDGE = 256
FIELD_EDGE = EDGE + REACH
WIDE = CELLS + 2 * EDGE
WIDE_BLOCKS = WIDE // LANES
SOLVED = WIDE_BLOCKS - 2
TILES = 9
INNER_LO = FIELD_EDGE // LANES
INNER = (CELLS - 2 * REACH) // LANES
MATRIX = 8
HALF = WIDE // 2
SENT = WIDE - LANES
BANDS = 3
HALO_ROWS = 56
COUPLING = 0.5

MIB = 1024 * 1024

f32 = jnp.float32
bf16 = jnp.bfloat16


def pack_fields(dst, dst_col, src, src_col, count):
    d = slice(dst_col, dst_col + count)
    s = slice(src_col, src_col + count)
    for field in range(3):
        dst[8 * field : 8 * field + 8, d] = src[field, 0:8, s]
        dst[24 + 4 * field : 28 + 4 * field, d] = src[field, 8:12, s]
    dst[36:40, d] = jnp.zeros((4, count), f32)


def halo_kernel(*refs):
    group, coef, *sources = refs[:9]
    head, tail, coef_row = refs[9:12]
    buffers, coef_here, sems = refs[12:26], refs[26], refs[27]
    copies = []
    for side, (field_col, col) in enumerate(((0, 0), (CELLS - FIELD_EDGE, CELLS - EDGE))):
        for n, source in enumerate(sources):
            cells = pl.ds(field_col, FIELD_EDGE) if n == 0 else pl.ds(col, EDGE)
            part = source.at[:, cells] if n > 2 else source.at[:, :, cells]
            copies.append(pltpu.make_async_copy(part, buffers[7 * side + n], sems.at[7 * side + n]))
    copies.append(pltpu.make_async_copy(coef, coef_here, sems.at[14]))
    for copy in copies:
        copy.start()
    for side, (out, col) in enumerate(((head, 0), (tail, CELLS - EDGE))):
        for copy in copies[7 * side : 7 * side + 7]:
            copy.wait()
        fields, index, weight, nbr, lap, ex, ey = buffers[7 * side : 7 * side + 7]
        pack_fields(out, 0, fields, 0, FIELD_EDGE)
        own = col + lax.broadcasted_iota(jnp.int32, (1, EDGE), 1)
        for p in range(POINTS):
            out[40 + p : 41 + p, 0:EDGE] = (index[p] - REACH - own).astype(f32)
            out[40 + p : 41 + p, EDGE : 2 * EDGE] = weight[p]
        away = (nbr[...] - NBR_REACH - own).astype(f32)
        out[52:56, 0:EDGE] = away[0:4]
        out[52:56, EDGE : 2 * EDGE] = lap[0:4]
        out[40:46, 2 * EDGE :] = ex[...]
        out[46:52, 2 * EDGE :] = ey[...]
        out[52:54, 2 * EDGE :] = away[4:6]
        out[54:56, 2 * EDGE :] = lap[4:6]
    copies[14].wait()
    lane = lax.broadcasted_iota(jnp.int32, (1, LANES), 1)
    row = jnp.zeros((1, LANES), f32)
    for k in range(ROWS):
        row = jnp.where(lane == group[0] * ROWS + k, coef_here[k], row)
    coef_row[...] = row


def split(v):
    high = v.astype(bf16)
    return high, (v - high.astype(f32)).astype(bf16)


def split_tiles(dst, first, src, src_col, count):
    for t in range(count):
        high, low = split(src[0:40, src_col + t * LANES : src_col + (t + 1) * LANES])
        dst[first + t, :, 0:LANES] = high
        dst[first + t, :, LANES:] = low


def stencil_block(x, slabs, first, col, away, weight, away_col):
    groups = 5
    acc = [jnp.zeros((8, LANES), f32) for _ in range(groups)]
    lane = lax.broadcasted_iota(jnp.int32, (1, LANES), 1)
    slot = lax.broadcasted_iota(jnp.int32, (LANES, LANES), 0).astype(bf16)
    ones = jnp.ones((LANES, LANES), bf16)
    near = slabs[pl.ds(first, TILES)].reshape(TILES * 8 * groups, 2 * LANES)

    def locate(p):
        at = away[p, :, pl.ds(away_col, LANES)] + (lane + REACH)
        w = jnp.broadcast_to(weight[p, :, pl.ds(away_col, LANES)], (8, LANES))
        return at & (LANES - 1), jnp.broadcast_to(at >> 7, (8, LANES)), w

    def add(part, tile, w):
        picked = [None] * groups
        for t in range(TILES):
            mask = tile == t
            for g in range(groups):
                picked[g] = part(t, g) if t == 0 else jnp.where(mask, part(t, g), picked[g])
        for g in range(groups):
            acc[g] = acc[g] + w * picked[g]

    def one_hot(inside):
        at = jnp.broadcast_to(inside.astype(f32), (LANES, LANES)).astype(bf16)
        return jnp.where(slot == at, ones, jnp.zeros_like(ones))

    def gathered(p):
        inside, tile, w = locate(p)
        inside = jnp.broadcast_to(inside, (8, LANES))

        def part(t, g):
            rows = x[8 * g : 8 * g + 8, pl.ds(col + t * LANES, LANES)]
            return jnp.take_along_axis(rows, inside, axis=1, mode="promise_in_bounds")

        add(part, tile, w)

    plain = list(range(MATRIX, POINTS))
    for pair in range(0, MATRIX, 2):
        points = [locate(p) for p in (pair, pair + 1)]
        hot = jnp.concatenate([one_hot(inside) for inside, _, _ in points], axis=1)
        rows = jnp.dot(near, jnp.concatenate([hot, hot], axis=0), preferred_element_type=f32)
        if plain:
            gathered(plain.pop(0))
        for i, (_, tile, w) in enumerate(points):
            c = slice(i * LANES, (i + 1) * LANES)
            add(lambda t, g: rows[40 * t + 8 * g : 40 * t + 8 * g + 8, c], tile, w)
    for p in plain:
        gathered(p)
    return acc


def right_side_block(up, up_col, side, side_x, side_y, col):
    lane = lax.broadcasted_iota(jnp.int32, (1, LANES), 1)
    upper = lax.broadcasted_iota(jnp.int32, (8, LANES), 0) < 4
    rows = (0, 8, 24)
    here = [up[r : r + 8, pl.ds(up_col + LANES, LANES)] for r in rows]
    acc = [jnp.zeros((8, LANES), f32) for _ in rows]
    for k in range(SIDES):
        at = jnp.broadcast_to(side[k : k + 1, pl.ds(col, LANES)] + (lane + LANES), (8, LANES))
        inside = at & (LANES - 1)
        tile = at >> 7
        wx = jnp.broadcast_to(side_x[k : k + 1, pl.ds(col, LANES)], (8, LANES))
        wy = jnp.broadcast_to(side_y[k : k + 1, pl.ds(col, LANES)], (8, LANES))
        weights = (wx, wy, jnp.where(upper, wx, wy))
        for g, r in enumerate(rows):
            picked = None
            for t in range(3):
                part = up[r : r + 8, pl.ds(up_col + t * LANES, LANES)]
                part = jnp.take_along_axis(part, inside, axis=1, mode="promise_in_bounds")
                picked = part if t == 0 else jnp.where(tile == t, part, picked)
            acc[g] = acc[g] + weights[g] * (picked - here[g])
    top = up[16:24, pl.ds(up_col + LANES, LANES)] - COUPLING * (acc[0] + acc[1])
    rest = up[32:36, pl.ds(up_col + LANES, LANES)] - COUPLING * (acc[2][0:4] + acc[2][4:8])
    return top, rest


def inner_kernel(
    fields, index, weight, nbr, ex, ey, coef_row,
    packed, slabs, upstream, right, away, side,
):
    pack_fields(packed, 0, fields, 0, CELLS)
    packed[36:37, 0:LANES] = coef_row[...]
    split_tiles(slabs, 0, packed, 0, CELLS // LANES)
    own = lax.broadcasted_iota(jnp.int32, (1, CELLS), 1)
    for p in range(POINTS):
        away[p] = index[p] - REACH - own
    side[...] = nbr[...] - NBR_REACH - own

    def stencil(b, carry):
        col = pl.multiple_of(b * LANES, LANES)
        acc = stencil_block(
            packed, slabs, b, col, away, weight, pl.multiple_of(col + REACH, LANES)
        )
        for g in range(5):
            upstream[8 * g : 8 * g + 8, pl.ds(col, LANES)] = acc[g]
        return carry

    lax.fori_loop(0, INNER, stencil, 0, unroll=4)

    def finish(b, carry):
        col = pl.multiple_of(b * LANES, LANES)
        top, rest = right_side_block(
            upstream, col, side, ex, ey, pl.multiple_of(col + REACH + LANES, LANES)
        )
        right[0:8, pl.ds(col, LANES)] = top
        right[8:12, pl.ds(col, LANES)] = rest
        return carry

    lax.fori_loop(0, INNER - 2, finish, 0, unroll=2)


def outer_kernel(
    packed, own_slabs, inner, inner_right, left, right, index, weight, nbr, ex, ey,
    winds, send, x, slabs, up, away, w_all, side, side_x, side_y, rs, rest_rs,
):
    halo_tiles = FIELD_EDGE // LANES
    x[:, 0:FIELD_EDGE] = left[0:40, :]
    x[:, FIELD_EDGE : FIELD_EDGE + CELLS] = packed[...]
    x[:, FIELD_EDGE + CELLS :] = right[0:40, :]
    split_tiles(slabs, 0, left, 0, halo_tiles)
    slabs[halo_tiles : halo_tiles + CELLS // LANES] = own_slabs[...]
    split_tiles(slabs, halo_tiles + CELLS // LANES, right, 0, halo_tiles)
    own = lax.broadcasted_iota(jnp.int32, (1, CELLS), 1)
    mid = slice(EDGE, EDGE + CELLS)
    for halo, cells in ((left, slice(0, EDGE)), (right, slice(EDGE + CELLS, WIDE))):
        for p in range(POINTS):
            away[p, :, cells] = halo[40 + p : 41 + p, 0:EDGE].astype(jnp.int32)
            w_all[p, :, cells] = halo[40 + p : 41 + p, EDGE : 2 * EDGE]
        side[0:4, cells] = halo[52:56, 0:EDGE].astype(jnp.int32)
        side[4:6, cells] = halo[52:54, 2 * EDGE :].astype(jnp.int32)
        side_x[:, cells] = halo[40:46, 2 * EDGE :]
        side_y[:, cells] = halo[46:52, 2 * EDGE :]
    for start in (0, CELLS - REACH):
        there = start + lax.broadcasted_iota(jnp.int32, (1, REACH), 1)
        cells = slice(EDGE + start, EDGE + start + REACH)
        for p in range(POINTS):
            away[p, :, cells] = index[p, :, start : start + REACH] - REACH - there
            w_all[p, :, cells] = weight[p, :, start : start + REACH]
    side[:, mid] = nbr[...] - NBR_REACH - own
    side_x[:, mid] = ex[...]
    side_y[:, mid] = ey[...]

    up[:, 0:LANES] = jnp.zeros((40, LANES), f32)
    up[:, LANES + WIDE :] = jnp.zeros((40, LANES), f32)
    first = LANES * (1 + INNER_LO)
    up[:, first : first + INNER * LANES] = inner[...]

    def stencil(i, carry):
        for b in (i, i + INNER_LO + INNER):
            col = pl.multiple_of(b * LANES, LANES)
            acc = stencil_block(x, slabs, b, col, away, w_all, col)
            for g in range(5):
                up[8 * g : 8 * g + 8, pl.ds(col + LANES, LANES)] = acc[g]
        return carry

    lax.fori_loop(0, INNER_LO, stencil, 0, unroll=3)

    for field in range(2):
        cells = slice(LANES + EDGE, LANES + EDGE + CELLS)
        winds[field, 0:8, :] = up[8 * field : 8 * field + 8, cells]
        winds[field, 8:12, :] = up[24 + 4 * field : 28 + 4 * field, cells]

    first = (INNER_LO + 1) * LANES
    last = first + (INNER - 2) * LANES
    rs[:, first:last] = inner_right[0:8, :]
    rest_rs[0:4, HALF + first : HALF + last] = inner_right[8:12, :]
    rest_rs[4:8, first:last] = inner_right[8:12, :]

    def finish(i, carry):
        for b in (i, i + INNER_LO + INNER - 1):
            col = pl.multiple_of(b * LANES, LANES)
            top, rest = right_side_block(up, col, side, side_x, side_y, col)
            rs[:, pl.ds(col, LANES)] = top
            rest_rs[0:4, pl.ds(col + HALF, LANES)] = rest
            rest_rs[4:8, pl.ds(col, LANES)] = rest
        return carry

    lax.fori_loop(0, INNER_LO + 1, finish, 0)

    lane = lax.broadcasted_iota(jnp.int32, (1, LANES), 1)
    start, end = slice(0, LANES), slice(WIDE - LANES, WIDE)
    rs[:, start] = jnp.where(lane < NBR_REACH, rs[:, end], rs[:, start])
    start, end = slice(HALF, HALF + LANES), slice(2 * HALF - LANES, 2 * HALF)
    rest_rs[0:4, start] = jnp.where(lane < NBR_REACH, rest_rs[4:8, end], rest_rs[0:4, start])
    rest_rs[4:5, end] = packed[36:37, 0:LANES]
    for j in range(GROUPS):
        send[j, :, 0:SENT] = rs[:, 0:SENT]
        send[j, :, SENT:] = rest_rs[:, HALF : 2 * HALF]


def band_kernel(left, right, nbr, lap, *refs):
    *matrices, total, side, side_w = refs

    own = lax.broadcasted_iota(jnp.int32, (1, CELLS), 1)
    mid = slice(EDGE, EDGE + CELLS)
    for halo, cells in ((left, slice(0, EDGE)), (right, slice(EDGE + CELLS, WIDE))):
        side[0:4, cells] = halo[52:56, 0:EDGE].astype(jnp.int32)
        side[4:6, cells] = halo[52:54, 2 * EDGE :].astype(jnp.int32)
        side_w[0:4, cells] = halo[52:56, EDGE : 2 * EDGE]
        side_w[4:6, cells] = halo[54:56, 2 * EDGE :]
    side[:, mid] = nbr[...] - NBR_REACH - own
    side_w[:, mid] = lap[...]
    total[...] = jnp.sum(side_w[...], axis=0, keepdims=True)
    lane = lax.broadcasted_iota(jnp.int32, (1, LANES), 1)
    slot = lax.broadcasted_iota(jnp.int32, (2 * LANES, LANES), 0)

    per = SOLVED // BANDS
    for part, matrix in enumerate(matrices):

        def block(b, carry):
            cells = pl.ds(pl.multiple_of((part * per + b + 1) * LANES, LANES), LANES)
            dense = jnp.zeros((2 * LANES, LANES), f32)
            for k in range(SIDES):
                at = side[k : k + 1, cells] + (lane + NBR_REACH)
                dense = dense + jnp.where(slot == at, side_w[k : k + 1, cells], 0.0)
            high, low = split(dense)
            matrix[b, :, 0:LANES] = high
            matrix[b, :, LANES:] = low
            return carry

        lax.fori_loop(0, per, block, 0)


def solve_kernel(
    got, total, to_first, to_second, from_rows, *refs
):
    matrices, (out, x, rhs, scaled, parts, others, last) = refs[:BANDS], refs[BANDS:]
    per = SOLVED // BANDS
    modes = GROUPS * ROWS
    lane = lax.broadcasted_iota(jnp.int32, (1, LANES), 1)
    coef_row = jnp.sum(got[:, 4, SENT + HALF - LANES :], axis=0, keepdims=True)
    eye = lax.broadcasted_iota(jnp.int32, (modes, LANES), 0) == lax.broadcasted_iota(
        jnp.int32, (modes, LANES), 1
    )
    coef = jnp.sum(jnp.where(eye, coef_row, 0.0), axis=1, keepdims=True)
    radius = 6.0 * coef / (1.0 + 6.0 * coef)
    steps = [
        1.0 / (1.0 + radius * math.cos(math.pi * (2 * s + 1) / (2.0 * SWEEPS)))
        for s in range(SWEEPS)
    ]
    dot = functools.partial(jnp.dot, preferred_element_type=f32)

    def keep(dst, b, v):
        both = jnp.concatenate(split(pltpu.roll(v, NBR_REACH, 1)), axis=0)
        for d in dst:
            d[b or SOLVED + 1, :, NBR_REACH:] = both[:, NBR_REACH:]
            d[b + 1, :, 0:NBR_REACH] = both[:, 0:NBR_REACH]

    half = WIDE_BLOCKS // 2
    transforms = [jnp.concatenate(split(m[...]), axis=0) for m in (to_first, to_second)]
    for b in range(SOLVED + 1):
        cols = slice(b * LANES, (b + 1) * LANES)
        rest = SENT + b % half * LANES
        levels = jnp.concatenate(
            [
                got[:, :, cols].reshape(GROUPS * 8, LANES),
                got[:, :, rest : rest + LANES].reshape(GROUPS * 8, LANES),
            ],
            axis=0,
        )
        four = dot(transforms[b // half], jnp.concatenate(split(levels), axis=1))
        full = four[:modes, :LANES] + (
            four[modes:, :LANES] + four[:modes, LANES:] + four[modes:, LANES:]
        )
        weight = total[:, cols]
        if b == 0:
            weight = jnp.where(lane < NBR_REACH, total[:, SENT:], weight)
        inverse = 1.0 / (1.0 + coef * weight)
        full = full * inverse
        rhs[b] = full
        scaled[b] = coef * inverse
        full = steps[0] * full
        x[b] = full
        keep((parts, others) if b == 0 else (parts,), b, full)

    def swept(source, sweep, b):
        four = dot(
            jnp.concatenate([source[b], source[b + 1]], axis=1), matrices[(b - 1) // per][(b - 1) % per]
        )
        moved = four[:modes, :LANES] + (
            four[modes:, :LANES] + four[:modes, LANES:] + four[modes:, LANES:]
        )
        return (1.0 - steps[sweep]) * x[b] + steps[sweep] * (rhs[b] + scaled[b] * moved)

    for sweep, source, target in ((1, parts, others), (2, others, parts)):
        for b in range(1, SOLVED + 1):
            fresh = swept(source, sweep, b)
            x[b] = fresh
            keep((target,), b, fresh)
    first = EDGE // LANES
    for i in range(CELLS // LANES):
        both = jnp.concatenate(split(swept(parts, 3, first + i)), axis=0)
        last[i // 2, :, i % 2 * LANES : (i % 2 + 1) * LANES] = both
    back = jnp.concatenate(split(from_rows[...]), axis=0)
    for i in range(CELLS // (2 * LANES)):
        both = dot(back, last[i])
        out[:, 2 * i * LANES : 2 * (i + 1) * LANES] = both[0:ROWS] + both[16 : 16 + ROWS]


def slab_order(matrix):
    groups = matrix.reshape(GROUPS, ROWS, -1)
    main = groups[:, 0:8].reshape(GROUPS * 8, -1)
    pads = (((0, 0), (0, 4), (0, 0)), ((0, 0), (4, 0), (0, 0)))
    return [
        jnp.concatenate([main, jnp.pad(groups[:, 8:12], pad).reshape(GROUPS * 8, -1)], axis=0)
        for pad in pads
    ]


def call(kernel, outs, scratch=(), name=None, spaces="", out_spaces="", vmem=32):
    kinds = {"s": pltpu.SMEM, "h": pltpu.HBM, "v": pltpu.VMEM}
    in_specs = [pl.BlockSpec(memory_space=kinds[k]) for k in spaces]
    shapes = [jax.ShapeDtypeStruct(s, d) for s, d in outs]
    specs = [pl.BlockSpec(memory_space=kinds[k]) for k in out_spaces or "v" * len(outs)]
    if len(outs) == 1:
        shapes, specs = shapes[0], specs[0]
    return pl.pallas_call(
        kernel,
        out_shape=shapes,
        in_specs=in_specs,
        out_specs=specs,
        scratch_shapes=list(scratch),
        name=name,
        compiler_params=pltpu.CompilerParams(vmem_limit_bytes=int(vmem * MIB)),
    )


def per_device(
    fields,
    stencil_index,
    stencil_weight,
    neighbours,
    lap_weight,
    edge_x,
    edge_y,
    to_modes,
    from_modes,
    helm_coef,
):
    patches = lax.axis_size("patch")
    group = lax.axis_index("lev")
    halo = ((HALO_ROWS, FIELD_EDGE), f32)
    buffers = [
        pltpu.VMEM((3, ROWS, FIELD_EDGE), f32),
        pltpu.VMEM((POINTS, 1, EDGE), jnp.int32),
        pltpu.VMEM((POINTS, 1, EDGE), f32),
        pltpu.VMEM((SIDES, EDGE), jnp.int32),
    ] + [pltpu.VMEM((SIDES, EDGE), f32)] * 3
    head, tail, coef_row = call(
        halo_kernel,
        [halo, halo, ((1, LANES), f32)],
        buffers * 2 + [pltpu.SMEM((ROWS,), f32), pltpu.SemaphoreType.DMA((15,))],
        name="halo",
        spaces="s" + 8 * "h",
        vmem=60,
    )(
        group[None], helm_coef, fields, stencil_index, stencil_weight, neighbours, lap_weight,
        edge_x, edge_y,
    )
    left = lax.ppermute(tail, "patch", [(i, (i + 1) % patches) for i in range(patches)])
    right = lax.ppermute(head, "patch", [((i + 1) % patches, i) for i in range(patches)])
    tiles = CELLS // LANES
    packed, slabs, inner, inner_right = call(
        inner_kernel,
        [
            ((40, CELLS), f32),
            ((tiles, 40, 2 * LANES), bf16),
            ((40, INNER * LANES), f32),
            ((ROWS, (INNER - 2) * LANES), f32),
        ],
        [pltpu.VMEM((POINTS, 1, CELLS), jnp.int32), pltpu.VMEM((SIDES, CELLS), jnp.int32)],
        name="inner",
        spaces=7 * "v",
    )(fields, stencil_index, stencil_weight, neighbours, edge_x, edge_y, coef_row)
    new_winds, send = call(
        outer_kernel,
        [((2, ROWS, CELLS), f32), ((GROUPS, 8, SENT + HALF), f32)],
        [
            pltpu.VMEM((40, CELLS + 2 * FIELD_EDGE), f32),
            pltpu.VMEM((tiles + 2 * FIELD_EDGE // LANES, 40, 2 * LANES), bf16),
            pltpu.VMEM((40, WIDE + 2 * LANES), f32),
            pltpu.VMEM((POINTS, 1, WIDE), jnp.int32),
            pltpu.VMEM((POINTS, 1, WIDE), f32),
            pltpu.VMEM((SIDES, WIDE), jnp.int32),
            pltpu.VMEM((SIDES, WIDE), f32),
            pltpu.VMEM((SIDES, WIDE), f32),
            pltpu.VMEM((8, WIDE), f32),
            pltpu.VMEM((8, WIDE + HALF), f32),
        ],
        name="outer",
        spaces=11 * "v",
    )(
        packed, slabs, inner, inner_right, left, right, stencil_index, stencil_weight,
        neighbours, edge_x, edge_y,
    )
    bands = ((SOLVED // BANDS, 2 * LANES, 2 * LANES), bf16)
    *matrices, total = call(
        band_kernel,
        [bands] * BANDS + [((1, WIDE), f32)],
        [pltpu.VMEM((SIDES, WIDE), jnp.int32), pltpu.VMEM((SIDES, WIDE), f32)],
        name="band",
        spaces=4 * "v",
    )(left, right, neighbours, lap_weight)
    got = lax.all_to_all(send, "lev", split_axis=0, concat_axis=0, tiled=True)
    to_slabs = [m.T for m in slab_order(to_modes.T)]
    from_rows = lax.dynamic_slice_in_dim(from_modes, group * ROWS, ROWS, 0)
    from_rows = jnp.pad(jnp.tile(from_rows, (1, 2)), ((0, 16 - ROWS), (0, 0)))
    modes = GROUPS * ROWS
    new_height = call(
        solve_kernel,
        [((ROWS, CELLS), f32)],
        [pltpu.VMEM((SOLVED + 1, modes, LANES), f32)] * 3
        + [pltpu.VMEM((SOLVED + 2, 2 * modes, LANES), bf16)] * 2
        + [
            pltpu.VMEM((CELLS // (2 * LANES), 2 * modes, 2 * LANES), bf16),
        ],
        name="solve",
        spaces=(5 + BANDS) * "v",
    )(got, total, *to_slabs, from_rows, *matrices)
    return new_winds, new_height


def solution(mesh):
    in_specs = (
        P(None, "lev", "patch"),
        P(None, "lev", "patch"),
        P(None, "lev", "patch"),
        P(None, "patch"),
        P(None, "patch"),
        P(None, "patch"),
        P(None, "patch"),
        P(),
        P(),
        P("lev"),
    )
    out_specs = (P(None, "lev", "patch"), P("lev", "patch"))
    return jax.shard_map(
        per_device, mesh=mesh, in_specs=in_specs, out_specs=out_specs, check_vma=False
    )
```

```python
import functools
import math

import jax
import jax.numpy as jnp
from jax import lax
from jax.experimental import pallas as pl
from jax.experimental.pallas import tpu as pltpu
from jax.sharding import PartitionSpec as P

CELLS = 2048
REACH = 512
NBR_REACH = 64
SWEEPS = 4
POINTS = 12
SIDES = 6
GROUPS = 8
ROWS = 12
LANES = 128
EDGE = 256
FIELD_EDGE = EDGE + REACH
WIDE = CELLS + 2 * EDGE
WIDE_BLOCKS = WIDE // LANES
SOLVED = WIDE_BLOCKS - 2
TILES = 9
INNER_LO = FIELD_EDGE // LANES
INNER = (CELLS - 2 * REACH) // LANES
MATRIX = 8
HALF = WIDE // 2
SENT = WIDE - LANES
BANDS = 6
HALO_ROWS = 56
COUPLING = 0.5

MIB = 1024 * 1024

f32 = jnp.float32
bf16 = jnp.bfloat16


def pack_fields(dst, dst_col, src, src_col, count):
    d = slice(dst_col, dst_col + count)
    s = slice(src_col, src_col + count)
    for field in range(3):
        dst[8 * field : 8 * field + 8, d] = src[field, 0:8, s]
        dst[24 + 4 * field : 28 + 4 * field, d] = src[field, 8:12, s]
    dst[36:40, d] = jnp.zeros((4, count), f32)


def halo_kernel(*refs):
    group, coef, *sources = refs[:9]
    head, tail, coef_row = refs[9:12]
    buffers, coef_here, sems = refs[12:26], refs[26], refs[27]
    copies = []
    for side, (field_col, col) in enumerate(((0, 0), (CELLS - FIELD_EDGE, CELLS - EDGE))):
        for n, source in enumerate(sources):
            cells = pl.ds(field_col, FIELD_EDGE) if n == 0 else pl.ds(col, EDGE)
            part = source.at[:, cells] if n > 2 else source.at[:, :, cells]
            copies.append(pltpu.make_async_copy(part, buffers[7 * side + n], sems.at[7 * side + n]))
    copies.append(pltpu.make_async_copy(coef, coef_here, sems.at[14]))
    for copy in copies:
        copy.start()
    for side, (out, col) in enumerate(((head, 0), (tail, CELLS - EDGE))):
        for copy in copies[7 * side : 7 * side + 7]:
            copy.wait()
        fields, index, weight, nbr, lap, ex, ey = buffers[7 * side : 7 * side + 7]
        pack_fields(out, 0, fields, 0, FIELD_EDGE)
        own = col + lax.broadcasted_iota(jnp.int32, (1, EDGE), 1)
        for p in range(POINTS):
            out[40 + p : 41 + p, 0:EDGE] = (index[p] - REACH - own).astype(f32)
            out[40 + p : 41 + p, EDGE : 2 * EDGE] = weight[p]
        away = (nbr[...] - NBR_REACH - own).astype(f32)
        out[52:56, 0:EDGE] = away[0:4]
        out[52:56, EDGE : 2 * EDGE] = lap[0:4]
        out[40:46, 2 * EDGE :] = ex[...]
        out[46:52, 2 * EDGE :] = ey[...]
        out[52:54, 2 * EDGE :] = away[4:6]
        out[54:56, 2 * EDGE :] = lap[4:6]
    copies[14].wait()
    lane = lax.broadcasted_iota(jnp.int32, (1, LANES), 1)
    row = jnp.zeros((1, LANES), f32)
    for k in range(ROWS):
        row = jnp.where(lane == group[0] * ROWS + k, coef_here[k], row)
    coef_row[...] = row


def split(v):
    high = v.astype(bf16)
    return high, (v - high.astype(f32)).astype(bf16)


def split_tiles(dst, first, src, src_col, count):
    for t in range(count):
        high, low = split(src[0:40, src_col + t * LANES : src_col + (t + 1) * LANES])
        dst[first + t, :, 0:LANES] = high
        dst[first + t, :, LANES:] = low


def stencil_block(x, col, slabs, slab, first, count, away, weight, matrix):
    groups = 5
    acc = [jnp.zeros((8, LANES), f32) for _ in range(groups)]
    lane = lax.broadcasted_iota(jnp.int32, (1, LANES), 1)
    slot = lax.broadcasted_iota(jnp.int32, (LANES, LANES), 0).astype(bf16)
    ones = jnp.ones((LANES, LANES), bf16)
    if matrix:
        near = slabs[pl.ds(slab, count)].reshape(count * 8 * groups, 2 * LANES)

    def locate(p):
        at = away(p) + (lane + REACH)
        w = jnp.broadcast_to(weight(p), (8, LANES))
        return at & (LANES - 1), jnp.broadcast_to(at >> 7, (8, LANES)), w

    def add(part, tile, w):
        picked = [None if count == TILES else jnp.zeros((8, LANES), f32)] * groups
        for t in range(count):
            mask = tile == first + t
            for g in range(groups):
                value = part(t, g)
                picked[g] = value if picked[g] is None else jnp.where(mask, value, picked[g])
        for g in range(groups):
            acc[g] = acc[g] + w * picked[g]

    def one_hot(inside):
        at = jnp.broadcast_to(inside.astype(f32), (LANES, LANES)).astype(bf16)
        return jnp.where(slot == at, ones, jnp.zeros_like(ones))

    def gathered(p):
        inside, tile, w = locate(p)
        inside = jnp.broadcast_to(inside, (8, LANES))

        def part(t, g):
            rows = x[8 * g : 8 * g + 8, pl.ds(col + t * LANES, LANES)]
            return jnp.take_along_axis(rows, inside, axis=1, mode="promise_in_bounds")

        add(part, tile, w)

    plain = list(range(matrix, POINTS))
    for pair in range(0, matrix, 2):
        points = [locate(p) for p in (pair, pair + 1)]
        hot = jnp.concatenate([one_hot(inside) for inside, _, _ in points], axis=1)
        rows = jnp.dot(near, jnp.concatenate([hot, hot], axis=0), preferred_element_type=f32)
        if plain:
            gathered(plain.pop(0))
        for i, (_, tile, w) in enumerate(points):
            c = slice(i * LANES, (i + 1) * LANES)
            add(lambda t, g: rows[40 * t + 8 * g : 40 * t + 8 * g + 8, c], tile, w)
    for p in plain:
        gathered(p)
    return acc


def own_points(index, weight, col):
    own = lax.broadcasted_iota(jnp.int32, (1, LANES), 1) + (col + REACH)
    cells = pl.ds(col, LANES)
    return lambda p: index[p, :, cells] - own, lambda p: weight[p, :, cells]


def right_side_block(up, up_col, side, side_x, side_y, col):
    lane = lax.broadcasted_iota(jnp.int32, (1, LANES), 1)
    upper = lax.broadcasted_iota(jnp.int32, (8, LANES), 0) < 4
    rows = (0, 8, 24)
    here = [up[r : r + 8, pl.ds(up_col + LANES, LANES)] for r in rows]
    acc = [jnp.zeros((8, LANES), f32) for _ in rows]
    for k in range(SIDES):
        at = jnp.broadcast_to(side[k : k + 1, pl.ds(col, LANES)] + (lane + LANES), (8, LANES))
        inside = at & (LANES - 1)
        tile = at >> 7
        wx = jnp.broadcast_to(side_x[k : k + 1, pl.ds(col, LANES)], (8, LANES))
        wy = jnp.broadcast_to(side_y[k : k + 1, pl.ds(col, LANES)], (8, LANES))
        weights = (wx, wy, jnp.where(upper, wx, wy))
        for g, r in enumerate(rows):
            picked = None
            for t in range(3):
                part = up[r : r + 8, pl.ds(up_col + t * LANES, LANES)]
                part = jnp.take_along_axis(part, inside, axis=1, mode="promise_in_bounds")
                picked = part if t == 0 else jnp.where(tile == t, part, picked)
            acc[g] = acc[g] + weights[g] * (picked - here[g])
    top = up[16:24, pl.ds(up_col + LANES, LANES)] - COUPLING * (acc[0] + acc[1])
    rest = up[32:36, pl.ds(up_col + LANES, LANES)] - COUPLING * (acc[2][0:4] + acc[2][4:8])
    return top, rest


def inner_kernel(
    fields, index, weight, nbr, ex, ey, coef_row,
    packed, slabs, upstream, right, side,
):
    pack_fields(packed, 0, fields, 0, CELLS)
    packed[36:37, 0:LANES] = coef_row[...]
    split_tiles(slabs, 0, packed, 0, CELLS // LANES)
    own = lax.broadcasted_iota(jnp.int32, (1, CELLS), 1)
    side[...] = nbr[...] - NBR_REACH - own
    tiles = CELLS // LANES
    reach = REACH // LANES

    def block(b, tile, first, count):
        col = b * LANES if isinstance(b, int) else pl.multiple_of(b * LANES, LANES)
        start = tile * LANES if isinstance(b, int) else pl.multiple_of(tile * LANES, LANES)
        away, points_weight = own_points(index, weight, col)
        acc = stencil_block(
            packed, start, slabs, tile, first, count, away, points_weight, MATRIX
        )
        for g in range(5):
            upstream[8 * g : 8 * g + 8, pl.ds(col, LANES)] = acc[g]

    def whole(i, carry):
        block(i + reach, i, 0, TILES)
        return carry

    lax.fori_loop(0, INNER, whole, 0, unroll=4)

    def finish(b, carry):
        col = pl.multiple_of((b + reach) * LANES, LANES)
        cells = pl.multiple_of(col + LANES, LANES)
        top, rest = right_side_block(upstream, col, side, ex, ey, cells)
        right[0:8, pl.ds(b * LANES, LANES)] = top
        right[8:12, pl.ds(b * LANES, LANES)] = rest
        return carry

    lax.fori_loop(0, INNER - 2, finish, 0, unroll=2)
    for b in range(reach):
        block(b, 0, reach - b, reach + 1 + b)
        block(tiles - 1 - b, tiles - 1 - b - reach, 0, reach + 1 + b)


def outer_kernel(
    packed, own_slabs, inner, inner_right, left, right, index, weight, own_side, ex, ey,
    winds, send, x, slabs, up, side, side_x, side_y, rs, rest_rs,
):
    halo_tiles = FIELD_EDGE // LANES
    reach = REACH // LANES
    edge = EDGE // LANES
    x[0, :, 0:FIELD_EDGE] = left[0:40, :]
    x[0, :, FIELD_EDGE:] = packed[:, 0:REACH]
    x[1, :, 0:REACH] = packed[:, CELLS - REACH :]
    x[1, :, REACH:] = right[0:40, :]
    split_tiles(slabs.at[0], 0, left, 0, halo_tiles)
    slabs[0, halo_tiles:] = own_slabs[0:reach]
    slabs[1, 0:reach] = own_slabs[CELLS // LANES - reach :]
    split_tiles(slabs.at[1], reach, right, 0, halo_tiles)
    mid = slice(EDGE, EDGE + CELLS)
    for halo, cells in ((left, slice(0, EDGE)), (right, slice(EDGE + CELLS, WIDE))):
        side[0:4, cells] = halo[52:56, 0:EDGE].astype(jnp.int32)
        side[4:6, cells] = halo[52:54, 2 * EDGE :].astype(jnp.int32)
        side_x[:, cells] = halo[40:46, 2 * EDGE :]
        side_y[:, cells] = halo[46:52, 2 * EDGE :]
    side[:, mid] = own_side[...]
    side_x[:, mid] = ex[...]
    side_y[:, mid] = ey[...]

    up[:, 0:LANES] = jnp.zeros((40, LANES), f32)
    up[:, LANES + WIDE :] = jnp.zeros((40, LANES), f32)
    up[:, LANES + EDGE : LANES + EDGE + CELLS] = inner[...]

    def halo_points(halo, col):
        cells = slice(col, col + LANES)
        far = slice(EDGE + col, EDGE + col + LANES)
        return (
            lambda p: halo[40 + p : 41 + p, cells].astype(jnp.int32),
            lambda p: halo[40 + p : 41 + p, far],
        )

    for b in range(halo_tiles):
        for s, halo in ((0, left), (1, right)):
            if b < edge:
                at = b if s == 0 else WIDE_BLOCKS - edge + b
                points = halo_points(halo, b * LANES)
                tile, first, count = b, 0, TILES
            else:
                count = halo_tiles - b
                at = b if s == 0 else WIDE_BLOCKS - 1 - b
                points = own_points(index, weight, (at - edge) * LANES)
                tile, first = (b, 0) if s == 0 else (reach, TILES - count)
            acc = stencil_block(
                x.at[s], tile * LANES, slabs.at[s], tile, first, count, *points,
                MATRIX if count > 2 else 0,
            )
            cells = slice((at + 1) * LANES, (at + 2) * LANES)
            for g in range(5):
                rows = slice(8 * g, 8 * g + 8)
                up[rows, cells] = acc[g] if b < edge else up[rows, cells] + acc[g]

    for field in range(2):
        cells = slice(LANES + EDGE, LANES + EDGE + CELLS)
        winds[field, 0:8, :] = up[8 * field : 8 * field + 8, cells]
        winds[field, 8:12, :] = up[24 + 4 * field : 28 + 4 * field, cells]

    first = (INNER_LO + 1) * LANES
    last = first + (INNER - 2) * LANES
    rs[:, first:last] = inner_right[0:8, :]
    rest_rs[0:4, HALF + first : HALF + last] = inner_right[8:12, :]
    rest_rs[4:8, first:last] = inner_right[8:12, :]

    def finish(i, carry):
        for b in (i, i + INNER_LO + INNER - 1):
            col = pl.multiple_of(b * LANES, LANES)
            top, rest = right_side_block(up, col, side, side_x, side_y, col)
            rs[:, pl.ds(col, LANES)] = top
            rest_rs[0:4, pl.ds(col + HALF, LANES)] = rest
            rest_rs[4:8, pl.ds(col, LANES)] = rest
        return carry

    lax.fori_loop(0, INNER_LO + 1, finish, 0)

    lane = lax.broadcasted_iota(jnp.int32, (1, LANES), 1)
    start, end = slice(0, LANES), slice(WIDE - LANES, WIDE)
    rs[:, start] = jnp.where(lane < NBR_REACH, rs[:, end], rs[:, start])
    start, end = slice(HALF, HALF + LANES), slice(2 * HALF - LANES, 2 * HALF)
    rest_rs[0:4, start] = jnp.where(lane < NBR_REACH, rest_rs[4:8, end], rest_rs[0:4, start])
    rest_rs[4:5, end] = packed[36:37, 0:LANES]
    for j in range(GROUPS):
        send[j, :, 0:SENT] = rs[:, 0:SENT]
        send[j, :, SENT:] = rest_rs[:, HALF : 2 * HALF]


def band_kernel(left, right, nbr, lap, *refs):
    *matrices, total, side, side_w = refs

    own = lax.broadcasted_iota(jnp.int32, (1, CELLS), 1)
    mid = slice(EDGE, EDGE + CELLS)
    for halo, cells in ((left, slice(0, EDGE)), (right, slice(EDGE + CELLS, WIDE))):
        side[0:4, cells] = halo[52:56, 0:EDGE].astype(jnp.int32)
        side[4:6, cells] = halo[52:54, 2 * EDGE :].astype(jnp.int32)
        side_w[0:4, cells] = halo[52:56, EDGE : 2 * EDGE]
        side_w[4:6, cells] = halo[54:56, 2 * EDGE :]
    side[:, mid] = nbr[...] - NBR_REACH - own
    side_w[:, mid] = lap[...]
    total[...] = jnp.sum(side_w[...], axis=0, keepdims=True)
    lane = lax.broadcasted_iota(jnp.int32, (1, LANES), 1)
    slot = lax.broadcasted_iota(jnp.int32, (2 * LANES, LANES), 0)

    per = SOLVED // BANDS
    for part, matrix in enumerate(matrices):

        def block(b, carry):
            cells = pl.ds(pl.multiple_of((part * per + b + 1) * LANES, LANES), LANES)
            dense = jnp.zeros((2 * LANES, LANES), f32)
            for k in range(SIDES):
                at = side[k : k + 1, cells] + (lane + NBR_REACH)
                dense = dense + jnp.where(slot == at, side_w[k : k + 1, cells], 0.0)
            high, low = split(dense)
            matrix[b, :, 0:LANES] = high
            matrix[b, :, LANES:] = low
            return carry

        lax.fori_loop(0, per, block, 0)


def solve_kernel(
    got, total, to_first, to_second, from_rows, *refs
):
    matrices, (out, x, rhs, scaled, parts, others, last) = refs[:BANDS], refs[BANDS:]
    per = SOLVED // BANDS
    modes = GROUPS * ROWS
    lane = lax.broadcasted_iota(jnp.int32, (1, LANES), 1)
    coef_row = jnp.sum(got[:, 4, SENT + HALF - LANES :], axis=0, keepdims=True)
    eye = lax.broadcasted_iota(jnp.int32, (modes, LANES), 0) == lax.broadcasted_iota(
        jnp.int32, (modes, LANES), 1
    )
    coef = jnp.sum(jnp.where(eye, coef_row, 0.0), axis=1, keepdims=True)
    radius = 6.0 * coef / (1.0 + 6.0 * coef)
    steps = [
        1.0 / (1.0 + radius * math.cos(math.pi * (2 * s + 1) / (2.0 * SWEEPS)))
        for s in range(SWEEPS)
    ]
    dot = functools.partial(jnp.dot, preferred_element_type=f32)

    def keep(dst, b, v):
        both = jnp.concatenate(split(pltpu.roll(v, NBR_REACH, 1)), axis=0)
        for d in dst:
            d[b or SOLVED + 1, :, NBR_REACH:] = both[:, NBR_REACH:]
            d[b + 1, :, 0:NBR_REACH] = both[:, 0:NBR_REACH]

    half = WIDE_BLOCKS // 2
    transforms = [jnp.concatenate(split(m[...]), axis=0) for m in (to_first, to_second)]
    for b in range(SOLVED + 1):
        cols = slice(b * LANES, (b + 1) * LANES)
        rest = SENT + b % half * LANES
        levels = jnp.concatenate(
            [
                got[:, :, cols].reshape(GROUPS * 8, LANES),
                got[:, :, rest : rest + LANES].reshape(GROUPS * 8, LANES),
            ],
            axis=0,
        )
        four = dot(transforms[b // half], jnp.concatenate(split(levels), axis=1))
        full = four[:modes, :LANES] + (
            four[modes:, :LANES] + four[:modes, LANES:] + four[modes:, LANES:]
        )
        weight = total[:, cols]
        if b == 0:
            weight = jnp.where(lane < NBR_REACH, total[:, SENT:], weight)
        inverse = 1.0 / (1.0 + coef * weight)
        full = full * inverse
        rhs[b] = full
        scaled[b] = coef * inverse
        full = steps[0] * full
        x[b] = full
        keep((parts, others) if b == 0 else (parts,), b, full)

    def swept(source, sweep, b):
        four = dot(
            jnp.concatenate([source[b], source[b + 1]], axis=1), matrices[(b - 1) // per][(b - 1) % per]
        )
        moved = four[:modes, :LANES] + (
            four[modes:, :LANES] + four[:modes, LANES:] + four[modes:, LANES:]
        )
        return (1.0 - steps[sweep]) * x[b] + steps[sweep] * (rhs[b] + scaled[b] * moved)

    for sweep, source, target in ((1, parts, others), (2, others, parts)):
        for b in range(1, SOLVED + 1):
            fresh = swept(source, sweep, b)
            x[b] = fresh
            keep((target,), b, fresh)
    first = EDGE // LANES
    for i in range(CELLS // LANES):
        both = jnp.concatenate(split(swept(parts, 3, first + i)), axis=0)
        last[i // 2, :, i % 2 * LANES : (i % 2 + 1) * LANES] = both
    back = jnp.concatenate(split(from_rows[...]), axis=0)
    for i in range(CELLS // (2 * LANES)):
        both = dot(back, last[i])
        out[:, 2 * i * LANES : 2 * (i + 1) * LANES] = both[0:ROWS] + both[16 : 16 + ROWS]


def slab_order(matrix):
    groups = matrix.reshape(GROUPS, ROWS, -1)
    main = groups[:, 0:8].reshape(GROUPS * 8, -1)
    pads = (((0, 0), (0, 4), (0, 0)), ((0, 0), (4, 0), (0, 0)))
    return [
        jnp.concatenate([main, jnp.pad(groups[:, 8:12], pad).reshape(GROUPS * 8, -1)], axis=0)
        for pad in pads
    ]


def call(kernel, outs, scratch=(), name=None, spaces="", out_spaces="", vmem=32):
    kinds = {"s": pltpu.SMEM, "h": pltpu.HBM, "v": pltpu.VMEM}
    in_specs = [pl.BlockSpec(memory_space=kinds[k]) for k in spaces]
    shapes = [jax.ShapeDtypeStruct(s, d) for s, d in outs]
    specs = [pl.BlockSpec(memory_space=kinds[k]) for k in out_spaces or "v" * len(outs)]
    if len(outs) == 1:
        shapes, specs = shapes[0], specs[0]
    return pl.pallas_call(
        kernel,
        out_shape=shapes,
        in_specs=in_specs,
        out_specs=specs,
        scratch_shapes=list(scratch),
        name=name,
        compiler_params=pltpu.CompilerParams(vmem_limit_bytes=int(vmem * MIB)),
    )


def per_device(
    fields,
    stencil_index,
    stencil_weight,
    neighbours,
    lap_weight,
    edge_x,
    edge_y,
    to_modes,
    from_modes,
    helm_coef,
):
    patches = lax.axis_size("patch")
    group = lax.axis_index("lev")
    halo = ((HALO_ROWS, FIELD_EDGE), f32)
    buffers = [
        pltpu.VMEM((3, ROWS, FIELD_EDGE), f32),
        pltpu.VMEM((POINTS, 1, EDGE), jnp.int32),
        pltpu.VMEM((POINTS, 1, EDGE), f32),
        pltpu.VMEM((SIDES, EDGE), jnp.int32),
    ] + [pltpu.VMEM((SIDES, EDGE), f32)] * 3
    head, tail, coef_row = call(
        halo_kernel,
        [halo, halo, ((1, LANES), f32)],
        buffers * 2 + [pltpu.SMEM((ROWS,), f32), pltpu.SemaphoreType.DMA((15,))],
        name="halo",
        spaces="s" + 8 * "h",
        vmem=60,
    )(
        group[None], helm_coef, fields, stencil_index, stencil_weight, neighbours, lap_weight,
        edge_x, edge_y,
    )
    left = lax.ppermute(tail, "patch", [(i, (i + 1) % patches) for i in range(patches)])
    right = lax.ppermute(head, "patch", [((i + 1) % patches, i) for i in range(patches)])
    tiles = CELLS // LANES
    packed, slabs, inner, inner_right, side = call(
        inner_kernel,
        [
            ((40, CELLS), f32),
            ((tiles, 40, 2 * LANES), bf16),
            ((40, CELLS), f32),
            ((ROWS, (INNER - 2) * LANES), f32),
            ((SIDES, CELLS), jnp.int32),
        ],
        name="inner",
        spaces=7 * "v",
    )(fields, stencil_index, stencil_weight, neighbours, edge_x, edge_y, coef_row)
    near = (FIELD_EDGE + REACH) // LANES
    new_winds, send = call(
        outer_kernel,
        [((2, ROWS, CELLS), f32), ((GROUPS, 8, SENT + HALF), f32)],
        [
            pltpu.VMEM((2, 40, near * LANES), f32),
            pltpu.VMEM((2, near, 40, 2 * LANES), bf16),
            pltpu.VMEM((40, WIDE + 2 * LANES), f32),
            pltpu.VMEM((SIDES, WIDE), jnp.int32),
            pltpu.VMEM((SIDES, WIDE), f32),
            pltpu.VMEM((SIDES, WIDE), f32),
            pltpu.VMEM((8, WIDE), f32),
            pltpu.VMEM((8, WIDE + HALF), f32),
        ],
        name="outer",
        spaces=11 * "v",
    )(
        packed, slabs, inner, inner_right, left, right, stencil_index, stencil_weight,
        side, edge_x, edge_y,
    )
    bands = ((SOLVED // BANDS, 2 * LANES, 2 * LANES), bf16)
    *matrices, total = call(
        band_kernel,
        [bands] * BANDS + [((1, WIDE), f32)],
        [pltpu.VMEM((SIDES, WIDE), jnp.int32), pltpu.VMEM((SIDES, WIDE), f32)],
        name="band",
        spaces=4 * "v",
    )(left, right, neighbours, lap_weight)
    got = lax.all_to_all(send, "lev", split_axis=0, concat_axis=0, tiled=True)
    to_slabs = [m.T for m in slab_order(to_modes.T)]
    from_rows = lax.dynamic_slice_in_dim(from_modes, group * ROWS, ROWS, 0)
    from_rows = jnp.pad(jnp.tile(from_rows, (1, 2)), ((0, 16 - ROWS), (0, 0)))
    modes = GROUPS * ROWS
    new_height = call(
        solve_kernel,
        [((ROWS, CELLS), f32)],
        [pltpu.VMEM((SOLVED + 1, modes, LANES), f32)] * 3
        + [pltpu.VMEM((SOLVED + 2, 2 * modes, LANES), bf16)] * 2
        + [
            pltpu.VMEM((CELLS // (2 * LANES), 2 * modes, 2 * LANES), bf16),
        ],
        name="solve",
        spaces=(5 + BANDS) * "v",
    )(got, total, *to_slabs, from_rows, *matrices)
    return new_winds, new_height


def solution(mesh):
    in_specs = (
        P(None, "lev", "patch"),
        P(None, "lev", "patch"),
        P(None, "lev", "patch"),
        P(None, "patch"),
        P(None, "patch"),
        P(None, "patch"),
        P(None, "patch"),
        P(),
        P(),
        P("lev"),
    )
    out_specs = (P(None, "lev", "patch"), P("lev", "patch"))
    return jax.shard_map(
        per_device, mesh=mesh, in_specs=in_specs, out_specs=out_specs, check_vma=False
    )
```

```python
import functools
import math

import jax
import jax.numpy as jnp
from jax import lax
from jax.experimental import pallas as pl
from jax.experimental.pallas import tpu as pltpu
from jax.sharding import PartitionSpec as P

CELLS = 2048
REACH = 512
NBR_REACH = 64
SWEEPS = 4
POINTS = 12
SIDES = 6
GROUPS = 8
ROWS = 12
LANES = 128
EDGE = 256
FIELD_EDGE = EDGE + REACH
WIDE = CELLS + 2 * EDGE
WIDE_BLOCKS = WIDE // LANES
SOLVED = WIDE_BLOCKS - 2
TILES = 9
INNER_LO = FIELD_EDGE // LANES
INNER = (CELLS - 2 * REACH) // LANES
MATRIX = 8
HALF = WIDE // 2
SENT = WIDE - LANES
BANDS = 5
NEAR = SOLVED // (BANDS + 1)
HALO_ROWS = 56
COUPLING = 0.5

MIB = 1024 * 1024

f32 = jnp.float32
bf16 = jnp.bfloat16


def pack_fields(dst, dst_col, src, src_col, count):
    d = slice(dst_col, dst_col + count)
    s = slice(src_col, src_col + count)
    for field in range(3):
        dst[8 * field : 8 * field + 8, d] = src[field, 0:8, s]
        dst[24 + 4 * field : 28 + 4 * field, d] = src[field, 8:12, s]
    dst[36:40, d] = jnp.zeros((4, count), f32)


def halo_kernel(*refs):
    group, coef, *sources = refs[:9]
    head, tail, coef_row = refs[9:12]
    buffers, coef_here, sems = refs[12:26], refs[26], refs[27]
    copies = []
    for side, (field_col, col) in enumerate(((0, 0), (CELLS - FIELD_EDGE, CELLS - EDGE))):
        for n, source in enumerate(sources):
            cells = pl.ds(field_col, FIELD_EDGE) if n == 0 else pl.ds(col, EDGE)
            part = source.at[:, cells] if n > 2 else source.at[:, :, cells]
            copies.append(pltpu.make_async_copy(part, buffers[7 * side + n], sems.at[7 * side + n]))
    copies.append(pltpu.make_async_copy(coef, coef_here, sems.at[14]))
    for copy in copies:
        copy.start()
    for side, (out, col) in enumerate(((head, 0), (tail, CELLS - EDGE))):
        for copy in copies[7 * side : 7 * side + 7]:
            copy.wait()
        fields, index, weight, nbr, lap, ex, ey = buffers[7 * side : 7 * side + 7]
        pack_fields(out, 0, fields, 0, FIELD_EDGE)
        own = col + lax.broadcasted_iota(jnp.int32, (1, EDGE), 1)
        for p in range(POINTS):
            out[40 + p : 41 + p, 0:EDGE] = (index[p] - REACH - own).astype(f32)
            out[40 + p : 41 + p, EDGE : 2 * EDGE] = weight[p]
        away = (nbr[...] - NBR_REACH - own).astype(f32)
        out[52:56, 0:EDGE] = away[0:4]
        out[52:56, EDGE : 2 * EDGE] = lap[0:4]
        out[40:46, 2 * EDGE :] = ex[...]
        out[46:52, 2 * EDGE :] = ey[...]
        out[52:54, 2 * EDGE :] = away[4:6]
        out[54:56, 2 * EDGE :] = lap[4:6]
    copies[14].wait()
    lane = lax.broadcasted_iota(jnp.int32, (1, LANES), 1)
    row = jnp.zeros((1, LANES), f32)
    for k in range(ROWS):
        row = jnp.where(lane == group[0] * ROWS + k, coef_here[k], row)
    coef_row[...] = row


def split(v):
    high = v.astype(bf16)
    return high, (v - high.astype(f32)).astype(bf16)


def split_tiles(dst, first, src, src_col, count):
    for t in range(count):
        high, low = split(src[0:40, src_col + t * LANES : src_col + (t + 1) * LANES])
        dst[first + t, :, 0:LANES] = high
        dst[first + t, :, LANES:] = low


def stencil_block(x, col, slabs, slab, first, count, away, weight, matrix):
    groups = 5
    acc = [jnp.zeros((8, LANES), f32) for _ in range(groups)]
    lane = lax.broadcasted_iota(jnp.int32, (1, LANES), 1)
    slot = lax.broadcasted_iota(jnp.int32, (LANES, LANES), 0).astype(bf16)
    ones = jnp.ones((LANES, LANES), bf16)
    if matrix:
        near = slabs[pl.ds(slab, count)].reshape(count * 8 * groups, 2 * LANES)

    def locate(p):
        at = away(p) + (lane + REACH)
        w = jnp.broadcast_to(weight(p), (8, LANES))
        return at & (LANES - 1), jnp.broadcast_to(at >> 7, (8, LANES)), w

    def add(part, tile, w):
        picked = [None if count == TILES else jnp.zeros((8, LANES), f32)] * groups
        for t in range(count):
            mask = tile == first + t
            for g in range(groups):
                value = part(t, g)
                picked[g] = value if picked[g] is None else jnp.where(mask, value, picked[g])
        for g in range(groups):
            acc[g] = acc[g] + w * picked[g]

    def one_hot(inside):
        at = jnp.broadcast_to(inside.astype(f32), (LANES, LANES)).astype(bf16)
        return jnp.where(slot == at, ones, jnp.zeros_like(ones))

    def gathered(p):
        inside, tile, w = locate(p)
        inside = jnp.broadcast_to(inside, (8, LANES))

        def part(t, g):
            rows = x[8 * g : 8 * g + 8, pl.ds(col + t * LANES, LANES)]
            return jnp.take_along_axis(rows, inside, axis=1, mode="promise_in_bounds")

        add(part, tile, w)

    plain = list(range(matrix, POINTS))
    for pair in range(0, matrix, 2):
        points = [locate(p) for p in (pair, pair + 1)]
        hot = jnp.concatenate([one_hot(inside) for inside, _, _ in points], axis=1)
        rows = jnp.dot(near, jnp.concatenate([hot, hot], axis=0), preferred_element_type=f32)
        if plain:
            gathered(plain.pop(0))
        for i, (_, tile, w) in enumerate(points):
            c = slice(i * LANES, (i + 1) * LANES)
            add(lambda t, g: rows[40 * t + 8 * g : 40 * t + 8 * g + 8, c], tile, w)
    for p in plain:
        gathered(p)
    return acc


def own_points(index, weight, col):
    own = lax.broadcasted_iota(jnp.int32, (1, LANES), 1) + (col + REACH)
    cells = pl.ds(col, LANES)
    return lambda p: index[p, :, cells] - own, lambda p: weight[p, :, cells]


def right_side_block(up, up_col, side, side_x, side_y, col):
    lane = lax.broadcasted_iota(jnp.int32, (1, LANES), 1)
    upper = lax.broadcasted_iota(jnp.int32, (8, LANES), 0) < 4
    rows = (0, 8, 24)
    here = [up[r : r + 8, pl.ds(up_col + LANES, LANES)] for r in rows]
    acc = [jnp.zeros((8, LANES), f32) for _ in rows]
    for k in range(SIDES):
        at = jnp.broadcast_to(side[k : k + 1, pl.ds(col, LANES)] + (lane + LANES), (8, LANES))
        inside = at & (LANES - 1)
        tile = at >> 7
        wx = jnp.broadcast_to(side_x[k : k + 1, pl.ds(col, LANES)], (8, LANES))
        wy = jnp.broadcast_to(side_y[k : k + 1, pl.ds(col, LANES)], (8, LANES))
        weights = (wx, wy, jnp.where(upper, wx, wy))
        for g, r in enumerate(rows):
            picked = None
            for t in range(3):
                part = up[r : r + 8, pl.ds(up_col + t * LANES, LANES)]
                part = jnp.take_along_axis(part, inside, axis=1, mode="promise_in_bounds")
                picked = part if t == 0 else jnp.where(tile == t, part, picked)
            acc[g] = acc[g] + weights[g] * (picked - here[g])
    top = up[16:24, pl.ds(up_col + LANES, LANES)] - COUPLING * (acc[0] + acc[1])
    rest = up[32:36, pl.ds(up_col + LANES, LANES)] - COUPLING * (acc[2][0:4] + acc[2][4:8])
    return top, rest


def inner_kernel(
    fields, index, weight, nbr, ex, ey, coef_row,
    packed, slabs, upstream, right, side,
):
    pack_fields(packed, 0, fields, 0, CELLS)
    packed[36:37, 0:LANES] = coef_row[...]
    split_tiles(slabs, 0, packed, 0, CELLS // LANES)
    own = lax.broadcasted_iota(jnp.int32, (1, CELLS), 1)
    side[...] = nbr[...] - NBR_REACH - own
    tiles = CELLS // LANES
    reach = REACH // LANES

    def block(b, tile, first, count):
        col = b * LANES if isinstance(b, int) else pl.multiple_of(b * LANES, LANES)
        start = tile * LANES if isinstance(b, int) else pl.multiple_of(tile * LANES, LANES)
        away, points_weight = own_points(index, weight, col)
        acc = stencil_block(
            packed, start, slabs, tile, first, count, away, points_weight, MATRIX
        )
        for g in range(5):
            upstream[8 * g : 8 * g + 8, pl.ds(col, LANES)] = acc[g]

    def whole(i, carry):
        block(i + reach, i, 0, TILES)
        return carry

    lax.fori_loop(0, INNER, whole, 0, unroll=4)

    def finish(b, carry):
        col = pl.multiple_of((b + reach) * LANES, LANES)
        cells = pl.multiple_of(col + LANES, LANES)
        top, rest = right_side_block(upstream, col, side, ex, ey, cells)
        right[0:8, pl.ds(b * LANES, LANES)] = top
        right[8:12, pl.ds(b * LANES, LANES)] = rest
        return carry

    lax.fori_loop(0, INNER - 2, finish, 0, unroll=2)
    for b in range(reach):
        block(b, 0, reach - b, reach + 1 + b)
        block(tiles - 1 - b, tiles - 1 - b - reach, 0, reach + 1 + b)


def outer_kernel(
    packed, own_slabs, inner, inner_right, left, right, index, weight, own_side, ex, ey,
    winds, send, x, slabs, up, side, side_x, side_y, rs, rest_rs,
):
    halo_tiles = FIELD_EDGE // LANES
    reach = REACH // LANES
    edge = EDGE // LANES
    x[0, :, 0:FIELD_EDGE] = left[0:40, :]
    x[0, :, FIELD_EDGE:] = packed[:, 0:REACH]
    x[1, :, 0:REACH] = packed[:, CELLS - REACH :]
    x[1, :, REACH:] = right[0:40, :]
    split_tiles(slabs.at[0], 0, left, 0, halo_tiles)
    slabs[0, halo_tiles:] = own_slabs[0:reach]
    slabs[1, 0:reach] = own_slabs[CELLS // LANES - reach :]
    split_tiles(slabs.at[1], reach, right, 0, halo_tiles)
    mid = slice(EDGE, EDGE + CELLS)
    for halo, cells in ((left, slice(0, EDGE)), (right, slice(EDGE + CELLS, WIDE))):
        side[0:4, cells] = halo[52:56, 0:EDGE].astype(jnp.int32)
        side[4:6, cells] = halo[52:54, 2 * EDGE :].astype(jnp.int32)
        side_x[:, cells] = halo[40:46, 2 * EDGE :]
        side_y[:, cells] = halo[46:52, 2 * EDGE :]
    side[:, mid] = own_side[...]
    side_x[:, mid] = ex[...]
    side_y[:, mid] = ey[...]

    up[:, 0:LANES] = jnp.zeros((40, LANES), f32)
    up[:, LANES + WIDE :] = jnp.zeros((40, LANES), f32)
    up[:, LANES + EDGE : LANES + EDGE + CELLS] = inner[...]

    def halo_points(halo, col):
        cells = slice(col, col + LANES)
        far = slice(EDGE + col, EDGE + col + LANES)
        return (
            lambda p: halo[40 + p : 41 + p, cells].astype(jnp.int32),
            lambda p: halo[40 + p : 41 + p, far],
        )

    for b in range(halo_tiles):
        for s, halo in ((0, left), (1, right)):
            if b < edge:
                at = b if s == 0 else WIDE_BLOCKS - edge + b
                points = halo_points(halo, b * LANES)
                tile, first, count = b, 0, TILES
            else:
                count = halo_tiles - b
                at = b if s == 0 else WIDE_BLOCKS - 1 - b
                points = own_points(index, weight, (at - edge) * LANES)
                tile, first = (b, 0) if s == 0 else (reach, TILES - count)
            acc = stencil_block(
                x.at[s], tile * LANES, slabs.at[s], tile, first, count, *points,
                MATRIX if count > 2 else 0,
            )
            cells = slice((at + 1) * LANES, (at + 2) * LANES)
            for g in range(5):
                rows = slice(8 * g, 8 * g + 8)
                up[rows, cells] = acc[g] if b < edge else up[rows, cells] + acc[g]

    for field in range(2):
        cells = slice(LANES + EDGE, LANES + EDGE + CELLS)
        winds[field, 0:8, :] = up[8 * field : 8 * field + 8, cells]
        winds[field, 8:12, :] = up[24 + 4 * field : 28 + 4 * field, cells]

    first = (INNER_LO + 1) * LANES
    last = first + (INNER - 2) * LANES
    rs[:, first:last] = inner_right[0:8, :]
    rest_rs[0:4, HALF + first : HALF + last] = inner_right[8:12, :]
    rest_rs[4:8, first:last] = inner_right[8:12, :]

    def finish(i, carry):
        for b in (i, i + INNER_LO + INNER - 1):
            col = pl.multiple_of(b * LANES, LANES)
            top, rest = right_side_block(up, col, side, side_x, side_y, col)
            rs[:, pl.ds(col, LANES)] = top
            rest_rs[0:4, pl.ds(col + HALF, LANES)] = rest
            rest_rs[4:8, pl.ds(col, LANES)] = rest
        return carry

    lax.fori_loop(0, INNER_LO + 1, finish, 0)

    lane = lax.broadcasted_iota(jnp.int32, (1, LANES), 1)
    start, end = slice(0, LANES), slice(WIDE - LANES, WIDE)
    rs[:, start] = jnp.where(lane < NBR_REACH, rs[:, end], rs[:, start])
    start, end = slice(HALF, HALF + LANES), slice(2 * HALF - LANES, 2 * HALF)
    rest_rs[0:4, start] = jnp.where(lane < NBR_REACH, rest_rs[4:8, end], rest_rs[0:4, start])
    rest_rs[4:5, end] = packed[36:37, 0:LANES]
    for j in range(GROUPS):
        send[j, :, 0:SENT] = rs[:, 0:SENT]
        send[j, :, SENT:] = rest_rs[:, HALF : 2 * HALF]


def band_block(side, weight, col):
    lane = lax.broadcasted_iota(jnp.int32, (1, LANES), 1)
    slot = lax.broadcasted_iota(jnp.int32, (2 * LANES, LANES), 0)
    cells = pl.ds(col, LANES)
    dense = jnp.zeros((2 * LANES, LANES), f32)
    for k in range(SIDES):
        at = side[k : k + 1, cells] + (lane + NBR_REACH)
        dense = dense + jnp.where(slot == at, weight[k : k + 1, cells], 0.0)
    return split(dense)


def band_kernel(left, right, nbr, lap, *refs):
    *matrices, near_side, near_weight, total, side, side_w = refs
    mid = slice(EDGE, EDGE + CELLS)
    for halo, cells in ((left, slice(0, EDGE)), (right, slice(EDGE + CELLS, WIDE))):
        side[0:4, cells] = halo[52:56, 0:EDGE].astype(jnp.int32)
        side[4:6, cells] = halo[52:54, 2 * EDGE :].astype(jnp.int32)
        side_w[0:4, cells] = halo[52:56, EDGE : 2 * EDGE]
        side_w[4:6, cells] = halo[54:56, 2 * EDGE :]
    own = lax.broadcasted_iota(jnp.int32, (1, CELLS), 1)
    side[:, mid] = nbr[...] - NBR_REACH - own
    side_w[:, mid] = lap[...]
    total[...] = jnp.sum(side_w[...], axis=0, keepdims=True)
    near_side[...] = side[:, LANES : (1 + NEAR) * LANES]
    near_weight[...] = side_w[:, LANES : (1 + NEAR) * LANES]
    for part, matrix in enumerate(matrices):

        def block(b, carry):
            col = pl.multiple_of(((part + 1) * NEAR + b + 1) * LANES, LANES)
            matrix[b, :, 0:LANES], matrix[b, :, LANES:] = band_block(side, side_w, col)
            return carry

        lax.fori_loop(0, NEAR, block, 0)


def solve_kernel(
    got, total, to_first, to_second, from_rows, *refs
):
    near_side, near_weight, *matrices = refs[: BANDS + 2]
    out, x, rhs, scaled, parts, others, last, held = refs[BANDS + 2 :]
    for b in range(NEAR):
        held[b, :, 0:LANES], held[b, :, LANES:] = band_block(near_side, near_weight, b * LANES)
    matrices = [held, *matrices]
    modes = GROUPS * ROWS
    lane = lax.broadcasted_iota(jnp.int32, (1, LANES), 1)
    coef_row = jnp.sum(got[:, 4, SENT + HALF - LANES :], axis=0, keepdims=True)
    eye = lax.broadcasted_iota(jnp.int32, (modes, LANES), 0) == lax.broadcasted_iota(
        jnp.int32, (modes, LANES), 1
    )
    coef = jnp.sum(jnp.where(eye, coef_row, 0.0), axis=1, keepdims=True)
    radius = 6.0 * coef / (1.0 + 6.0 * coef)
    steps = [
        1.0 / (1.0 + radius * math.cos(math.pi * (2 * s + 1) / (2.0 * SWEEPS)))
        for s in range(SWEEPS)
    ]
    dot = functools.partial(jnp.dot, preferred_element_type=f32)

    def keep(dst, b, v):
        both = jnp.concatenate(split(pltpu.roll(v, NBR_REACH, 1)), axis=0)
        for d in dst:
            d[b or SOLVED + 1, :, NBR_REACH:] = both[:, NBR_REACH:]
            d[b + 1, :, 0:NBR_REACH] = both[:, 0:NBR_REACH]

    half = WIDE_BLOCKS // 2
    transforms = [jnp.concatenate(split(m[...]), axis=0) for m in (to_first, to_second)]
    for b in range(SOLVED + 1):
        cols = slice(b * LANES, (b + 1) * LANES)
        rest = SENT + b % half * LANES
        levels = jnp.concatenate(
            [
                got[:, :, cols].reshape(GROUPS * 8, LANES),
                got[:, :, rest : rest + LANES].reshape(GROUPS * 8, LANES),
            ],
            axis=0,
        )
        four = dot(transforms[b // half], jnp.concatenate(split(levels), axis=1))
        full = four[:modes, :LANES] + (
            four[modes:, :LANES] + four[:modes, LANES:] + four[modes:, LANES:]
        )
        weight = total[:, cols]
        if b == 0:
            weight = jnp.where(lane < NBR_REACH, total[:, SENT:], weight)
        inverse = 1.0 / (1.0 + coef * weight)
        full = full * inverse
        rhs[b] = full
        scaled[b] = coef * inverse
        full = steps[0] * full
        x[b] = full
        keep((parts, others) if b == 0 else (parts,), b, full)

    def swept(source, sweep, b):
        four = dot(
            jnp.concatenate([source[b], source[b + 1]], axis=1), matrices[(b - 1) // NEAR][(b - 1) % NEAR]
        )
        moved = four[:modes, :LANES] + (
            four[modes:, :LANES] + four[:modes, LANES:] + four[modes:, LANES:]
        )
        return (1.0 - steps[sweep]) * x[b] + steps[sweep] * (rhs[b] + scaled[b] * moved)

    for sweep, source, target in ((1, parts, others), (2, others, parts)):
        for b in range(1, SOLVED + 1):
            fresh = swept(source, sweep, b)
            x[b] = fresh
            keep((target,), b, fresh)
    first = EDGE // LANES
    for i in range(CELLS // LANES):
        both = jnp.concatenate(split(swept(parts, 3, first + i)), axis=0)
        last[i // 2, :, i % 2 * LANES : (i % 2 + 1) * LANES] = both
    back = jnp.concatenate(split(from_rows[...]), axis=0)
    for i in range(CELLS // (2 * LANES)):
        both = dot(back, last[i])
        out[:, 2 * i * LANES : 2 * (i + 1) * LANES] = both[0:ROWS] + both[16 : 16 + ROWS]


def slab_order(matrix):
    groups = matrix.reshape(GROUPS, ROWS, -1)
    main = groups[:, 0:8].reshape(GROUPS * 8, -1)
    pads = (((0, 0), (0, 4), (0, 0)), ((0, 0), (4, 0), (0, 0)))
    return [
        jnp.concatenate([main, jnp.pad(groups[:, 8:12], pad).reshape(GROUPS * 8, -1)], axis=0)
        for pad in pads
    ]


def call(kernel, outs, scratch=(), name=None, spaces="", out_spaces="", vmem=32):
    kinds = {"s": pltpu.SMEM, "h": pltpu.HBM, "v": pltpu.VMEM}
    in_specs = [pl.BlockSpec(memory_space=kinds[k]) for k in spaces]
    shapes = [jax.ShapeDtypeStruct(s, d) for s, d in outs]
    specs = [pl.BlockSpec(memory_space=kinds[k]) for k in out_spaces or "v" * len(outs)]
    if len(outs) == 1:
        shapes, specs = shapes[0], specs[0]
    return pl.pallas_call(
        kernel,
        out_shape=shapes,
        in_specs=in_specs,
        out_specs=specs,
        scratch_shapes=list(scratch),
        name=name,
        compiler_params=pltpu.CompilerParams(vmem_limit_bytes=int(vmem * MIB)),
    )


def per_device(
    fields,
    stencil_index,
    stencil_weight,
    neighbours,
    lap_weight,
    edge_x,
    edge_y,
    to_modes,
    from_modes,
    helm_coef,
):
    patches = lax.axis_size("patch")
    group = lax.axis_index("lev")
    halo = ((HALO_ROWS, FIELD_EDGE), f32)
    buffers = [
        pltpu.VMEM((3, ROWS, FIELD_EDGE), f32),
        pltpu.VMEM((POINTS, 1, EDGE), jnp.int32),
        pltpu.VMEM((POINTS, 1, EDGE), f32),
        pltpu.VMEM((SIDES, EDGE), jnp.int32),
    ] + [pltpu.VMEM((SIDES, EDGE), f32)] * 3
    head, tail, coef_row = call(
        halo_kernel,
        [halo, halo, ((1, LANES), f32)],
        buffers * 2 + [pltpu.SMEM((ROWS,), f32), pltpu.SemaphoreType.DMA((15,))],
        name="halo",
        spaces="s" + 8 * "h",
        vmem=60,
    )(
        group[None], helm_coef, fields, stencil_index, stencil_weight, neighbours, lap_weight,
        edge_x, edge_y,
    )
    left = lax.ppermute(tail, "patch", [(i, (i + 1) % patches) for i in range(patches)])
    right = lax.ppermute(head, "patch", [((i + 1) % patches, i) for i in range(patches)])
    tiles = CELLS // LANES
    packed, slabs, inner, inner_right, side = call(
        inner_kernel,
        [
            ((40, CELLS), f32),
            ((tiles, 40, 2 * LANES), bf16),
            ((40, CELLS), f32),
            ((ROWS, (INNER - 2) * LANES), f32),
            ((SIDES, CELLS), jnp.int32),
        ],
        name="inner",
        spaces=7 * "v",
    )(fields, stencil_index, stencil_weight, neighbours, edge_x, edge_y, coef_row)
    near = (FIELD_EDGE + REACH) // LANES
    new_winds, send = call(
        outer_kernel,
        [((2, ROWS, CELLS), f32), ((GROUPS, 8, SENT + HALF), f32)],
        [
            pltpu.VMEM((2, 40, near * LANES), f32),
            pltpu.VMEM((2, near, 40, 2 * LANES), bf16),
            pltpu.VMEM((40, WIDE + 2 * LANES), f32),
            pltpu.VMEM((SIDES, WIDE), jnp.int32),
            pltpu.VMEM((SIDES, WIDE), f32),
            pltpu.VMEM((SIDES, WIDE), f32),
            pltpu.VMEM((8, WIDE), f32),
            pltpu.VMEM((8, WIDE + HALF), f32),
        ],
        name="outer",
        spaces=11 * "v",
    )(
        packed, slabs, inner, inner_right, left, right, stencil_index, stencil_weight,
        side, edge_x, edge_y,
    )
    bands = ((NEAR, 2 * LANES, 2 * LANES), bf16)
    near = (SIDES, NEAR * LANES)
    *matrices, near_side, near_weight, total = call(
        band_kernel,
        [bands] * BANDS + [(near, jnp.int32), (near, f32), ((1, WIDE), f32)],
        [pltpu.VMEM((SIDES, WIDE), jnp.int32), pltpu.VMEM((SIDES, WIDE), f32)],
        name="band",
        spaces=4 * "v",
    )(left, right, neighbours, lap_weight)
    got = lax.all_to_all(send, "lev", split_axis=0, concat_axis=0, tiled=True)
    to_slabs = [m.T for m in slab_order(to_modes.T)]
    from_rows = lax.dynamic_slice_in_dim(from_modes, group * ROWS, ROWS, 0)
    from_rows = jnp.pad(jnp.tile(from_rows, (1, 2)), ((0, 16 - ROWS), (0, 0)))
    modes = GROUPS * ROWS
    new_height = call(
        solve_kernel,
        [((ROWS, CELLS), f32)],
        [pltpu.VMEM((SOLVED + 1, modes, LANES), f32)] * 3
        + [pltpu.VMEM((SOLVED + 2, 2 * modes, LANES), bf16)] * 2
        + [
            pltpu.VMEM((CELLS // (2 * LANES), 2 * modes, 2 * LANES), bf16),
            pltpu.VMEM(*bands),
        ],
        name="solve",
        spaces=(7 + BANDS) * "v",
    )(got, total, *to_slabs, from_rows, near_side, near_weight, *matrices)
    return new_winds, new_height


def solution(mesh):
    in_specs = (
        P(None, "lev", "patch"),
        P(None, "lev", "patch"),
        P(None, "lev", "patch"),
        P(None, "patch"),
        P(None, "patch"),
        P(None, "patch"),
        P(None, "patch"),
        P(),
        P(),
        P("lev"),
    )
    out_specs = (P(None, "lev", "patch"), P("lev", "patch"))
    return jax.shard_map(
        per_device, mesh=mesh, in_specs=in_specs, out_specs=out_specs, check_vma=False
    )
```

```python
import functools
import math

import jax
import jax.numpy as jnp
from jax import lax
from jax.experimental import pallas as pl
from jax.experimental.pallas import tpu as pltpu
from jax.sharding import PartitionSpec as P

CELLS = 2048
REACH = 512
NBR_REACH = 64
SWEEPS = 4
POINTS = 12
SIDES = 6
GROUPS = 8
ROWS = 12
LANES = 128
EDGE = 256
FIELD_EDGE = EDGE + REACH
WIDE = CELLS + 2 * EDGE
WIDE_BLOCKS = WIDE // LANES
SOLVED = WIDE_BLOCKS - 2
TILES = 9
INNER_LO = FIELD_EDGE // LANES
INNER = (CELLS - 2 * REACH) // LANES
MATRIX = 8
HALF = WIDE // 2
SENT = WIDE - LANES
BANDS = 5
NEAR = SOLVED // (BANDS + 1)
HALO_ROWS = 56
COUPLING = 0.5

MIB = 1024 * 1024

f32 = jnp.float32
bf16 = jnp.bfloat16


def pack_fields(dst, dst_col, src, src_col, count):
    d = slice(dst_col, dst_col + count)
    s = slice(src_col, src_col + count)
    for field in range(3):
        dst[8 * field : 8 * field + 8, d] = src[field, 0:8, s]
        dst[24 + 4 * field : 28 + 4 * field, d] = src[field, 8:12, s]
    dst[36:40, d] = jnp.zeros((4, count), f32)


def halo_kernel(*refs):
    group, coef, *sources = refs[:9]
    head, tail, coef_row = refs[9:12]
    buffers, coef_here, sems, staged = refs[12:26], refs[26], refs[27], refs[28:30]
    sent = []
    copies = []
    for side, (field_col, col) in enumerate(((0, 0), (CELLS - FIELD_EDGE, CELLS - EDGE))):
        for n, source in enumerate(sources):
            cells = pl.ds(field_col, FIELD_EDGE) if n == 0 else pl.ds(col, EDGE)
            part = source.at[:, cells] if n > 2 else source.at[:, :, cells]
            copies.append(pltpu.make_async_copy(part, buffers[7 * side + n], sems.at[7 * side + n]))
    copies.append(pltpu.make_async_copy(coef, coef_here, sems.at[14]))
    for copy in copies:
        copy.start()
    for side, (far, col) in enumerate(((head, 0), (tail, CELLS - EDGE))):
        out = staged[side]
        for copy in copies[7 * side : 7 * side + 7]:
            copy.wait()
        fields, index, weight, nbr, lap, ex, ey = buffers[7 * side : 7 * side + 7]
        pack_fields(out, 0, fields, 0, FIELD_EDGE)
        own = col + lax.broadcasted_iota(jnp.int32, (1, EDGE), 1)
        for p in range(POINTS):
            out[40 + p : 41 + p, 0:EDGE] = (index[p] - REACH - own).astype(f32)
            out[40 + p : 41 + p, EDGE : 2 * EDGE] = weight[p]
        away = (nbr[...] - NBR_REACH - own).astype(f32)
        out[52:56, 0:EDGE] = away[0:4]
        out[52:56, EDGE : 2 * EDGE] = lap[0:4]
        out[40:46, 2 * EDGE :] = ex[...]
        out[46:52, 2 * EDGE :] = ey[...]
        out[52:54, 2 * EDGE :] = away[4:6]
        out[54:56, 2 * EDGE :] = lap[4:6]
        sent.append(pltpu.make_async_copy(out, far, sems.at[15 + side]))
        sent[side].start()
    copies[14].wait()
    lane = lax.broadcasted_iota(jnp.int32, (1, LANES), 1)
    row = jnp.zeros((1, LANES), f32)
    for k in range(ROWS):
        row = jnp.where(lane == group[0] * ROWS + k, coef_here[k], row)
    coef_row[...] = row
    for copy in sent:
        copy.wait()


def split(v):
    high = v.astype(bf16)
    return high, (v - high.astype(f32)).astype(bf16)


def split_tiles(dst, first, src, src_col, count):
    for t in range(count):
        high, low = split(src[0:40, src_col + t * LANES : src_col + (t + 1) * LANES])
        dst[first + t, :, 0:LANES] = high
        dst[first + t, :, LANES:] = low


def stencil_block(x, col, slabs, slab, first, count, away, weight, matrix):
    groups = 5
    acc = [jnp.zeros((8, LANES), f32) for _ in range(groups)]
    lane = lax.broadcasted_iota(jnp.int32, (1, LANES), 1)
    slot = lax.broadcasted_iota(jnp.int32, (LANES, LANES), 0).astype(bf16)
    ones = jnp.ones((LANES, LANES), bf16)
    if matrix:
        near = slabs[pl.ds(slab, count)].reshape(count * 8 * groups, 2 * LANES)

    def locate(p):
        at = away(p) + (lane + REACH)
        w = jnp.broadcast_to(weight(p), (8, LANES))
        return at & (LANES - 1), jnp.broadcast_to(at >> 7, (8, LANES)), w

    def add(part, tile, w):
        picked = [None if count == TILES else jnp.zeros((8, LANES), f32)] * groups
        for t in range(count):
            mask = tile == first + t
            for g in range(groups):
                value = part(t, g)
                picked[g] = value if picked[g] is None else jnp.where(mask, value, picked[g])
        for g in range(groups):
            acc[g] = acc[g] + w * picked[g]

    def one_hot(inside):
        at = jnp.broadcast_to(inside.astype(f32), (LANES, LANES)).astype(bf16)
        return jnp.where(slot == at, ones, jnp.zeros_like(ones))

    def gathered(p):
        inside, tile, w = locate(p)
        inside = jnp.broadcast_to(inside, (8, LANES))

        def part(t, g):
            rows = x[8 * g : 8 * g + 8, pl.ds(col + t * LANES, LANES)]
            return jnp.take_along_axis(rows, inside, axis=1, mode="promise_in_bounds")

        add(part, tile, w)

    plain = list(range(matrix, POINTS))
    for pair in range(0, matrix, 2):
        points = [locate(p) for p in (pair, pair + 1)]
        hot = jnp.concatenate([one_hot(inside) for inside, _, _ in points], axis=1)
        rows = jnp.dot(near, jnp.concatenate([hot, hot], axis=0), preferred_element_type=f32)
        if plain:
            gathered(plain.pop(0))
        for i, (_, tile, w) in enumerate(points):
            c = slice(i * LANES, (i + 1) * LANES)
            add(lambda t, g: rows[40 * t + 8 * g : 40 * t + 8 * g + 8, c], tile, w)
    for p in plain:
        gathered(p)
    return acc


def own_points(index, weight, col):
    own = lax.broadcasted_iota(jnp.int32, (1, LANES), 1) + (col + REACH)
    cells = pl.ds(col, LANES)
    return lambda p: index[p, :, cells] - own, lambda p: weight[p, :, cells]


def right_side_block(up, up_col, side, side_x, side_y, col):
    lane = lax.broadcasted_iota(jnp.int32, (1, LANES), 1)
    upper = lax.broadcasted_iota(jnp.int32, (8, LANES), 0) < 4
    rows = (0, 8, 24)
    here = [up[r : r + 8, pl.ds(up_col + LANES, LANES)] for r in rows]
    acc = [jnp.zeros((8, LANES), f32) for _ in rows]
    for k in range(SIDES):
        at = jnp.broadcast_to(side[k : k + 1, pl.ds(col, LANES)] + (lane + LANES), (8, LANES))
        inside = at & (LANES - 1)
        tile = at >> 7
        wx = jnp.broadcast_to(side_x[k : k + 1, pl.ds(col, LANES)], (8, LANES))
        wy = jnp.broadcast_to(side_y[k : k + 1, pl.ds(col, LANES)], (8, LANES))
        weights = (wx, wy, jnp.where(upper, wx, wy))
        for g, r in enumerate(rows):
            picked = None
            for t in range(3):
                part = up[r : r + 8, pl.ds(up_col + t * LANES, LANES)]
                part = jnp.take_along_axis(part, inside, axis=1, mode="promise_in_bounds")
                picked = part if t == 0 else jnp.where(tile == t, part, picked)
            acc[g] = acc[g] + weights[g] * (picked - here[g])
    top = up[16:24, pl.ds(up_col + LANES, LANES)] - COUPLING * (acc[0] + acc[1])
    rest = up[32:36, pl.ds(up_col + LANES, LANES)] - COUPLING * (acc[2][0:4] + acc[2][4:8])
    return top, rest


def inner_kernel(
    fields, index, weight, nbr, ex, ey, coef_row,
    packed, slabs, upstream, right, side,
):
    pack_fields(packed, 0, fields, 0, CELLS)
    packed[36:37, 0:LANES] = coef_row[...]
    split_tiles(slabs, 0, packed, 0, CELLS // LANES)
    own = lax.broadcasted_iota(jnp.int32, (1, CELLS), 1)
    side[...] = nbr[...] - NBR_REACH - own
    tiles = CELLS // LANES
    reach = REACH // LANES

    def block(b, tile, first, count):
        col = b * LANES if isinstance(b, int) else pl.multiple_of(b * LANES, LANES)
        start = tile * LANES if isinstance(b, int) else pl.multiple_of(tile * LANES, LANES)
        away, points_weight = own_points(index, weight, col)
        acc = stencil_block(
            packed, start, slabs, tile, first, count, away, points_weight, MATRIX
        )
        for g in range(5):
            upstream[8 * g : 8 * g + 8, pl.ds(col, LANES)] = acc[g]

    def whole(i, carry):
        block(i + reach, i, 0, TILES)
        return carry

    lax.fori_loop(0, INNER, whole, 0, unroll=4)

    def finish(b, carry):
        col = pl.multiple_of((b + reach) * LANES, LANES)
        cells = pl.multiple_of(col + LANES, LANES)
        top, rest = right_side_block(upstream, col, side, ex, ey, cells)
        right[0:8, pl.ds(b * LANES, LANES)] = top
        right[8:12, pl.ds(b * LANES, LANES)] = rest
        return carry

    lax.fori_loop(0, INNER - 2, finish, 0, unroll=2)
    for b in range(reach):
        block(b, 0, reach - b, reach + 1 + b)
        block(tiles - 1 - b, tiles - 1 - b - reach, 0, reach + 1 + b)


def outer_kernel(
    packed, own_slabs, inner, inner_right, left, right, index, weight, own_side, ex, ey,
    winds, send, x, slabs, up, side, side_x, side_y, rs, rest_rs,
):
    halo_tiles = FIELD_EDGE // LANES
    reach = REACH // LANES
    edge = EDGE // LANES
    x[0, :, 0:FIELD_EDGE] = left[0:40, :]
    x[0, :, FIELD_EDGE:] = packed[:, 0:REACH]
    x[1, :, 0:REACH] = packed[:, CELLS - REACH :]
    x[1, :, REACH:] = right[0:40, :]
    split_tiles(slabs.at[0], 0, left, 0, halo_tiles)
    slabs[0, halo_tiles:] = own_slabs[0:reach]
    slabs[1, 0:reach] = own_slabs[CELLS // LANES - reach :]
    split_tiles(slabs.at[1], reach, right, 0, halo_tiles)
    mid = slice(EDGE, EDGE + CELLS)
    for halo, cells in ((left, slice(0, EDGE)), (right, slice(EDGE + CELLS, WIDE))):
        side[0:4, cells] = halo[52:56, 0:EDGE].astype(jnp.int32)
        side[4:6, cells] = halo[52:54, 2 * EDGE :].astype(jnp.int32)
        side_x[:, cells] = halo[40:46, 2 * EDGE :]
        side_y[:, cells] = halo[46:52, 2 * EDGE :]
    side[:, mid] = own_side[...]
    side_x[:, mid] = ex[...]
    side_y[:, mid] = ey[...]

    up[:, 0:LANES] = jnp.zeros((40, LANES), f32)
    up[:, LANES + WIDE :] = jnp.zeros((40, LANES), f32)
    up[:, LANES + EDGE : LANES + EDGE + CELLS] = inner[...]

    def halo_points(halo, col):
        cells = slice(col, col + LANES)
        far = slice(EDGE + col, EDGE + col + LANES)
        return (
            lambda p: halo[40 + p : 41 + p, cells].astype(jnp.int32),
            lambda p: halo[40 + p : 41 + p, far],
        )

    for b in range(halo_tiles):
        for s, halo in ((0, left), (1, right)):
            if b < edge:
                at = b if s == 0 else WIDE_BLOCKS - edge + b
                points = halo_points(halo, b * LANES)
                tile, first, count = b, 0, TILES
            else:
                count = halo_tiles - b
                at = b if s == 0 else WIDE_BLOCKS - 1 - b
                points = own_points(index, weight, (at - edge) * LANES)
                tile, first = (b, 0) if s == 0 else (reach, TILES - count)
            acc = stencil_block(
                x.at[s], tile * LANES, slabs.at[s], tile, first, count, *points,
                MATRIX if count > 2 else 0,
            )
            cells = slice((at + 1) * LANES, (at + 2) * LANES)
            for g in range(5):
                rows = slice(8 * g, 8 * g + 8)
                up[rows, cells] = acc[g] if b < edge else up[rows, cells] + acc[g]

    for field in range(2):
        cells = slice(LANES + EDGE, LANES + EDGE + CELLS)
        winds[field, 0:8, :] = up[8 * field : 8 * field + 8, cells]
        winds[field, 8:12, :] = up[24 + 4 * field : 28 + 4 * field, cells]

    first = (INNER_LO + 1) * LANES
    last = first + (INNER - 2) * LANES
    rs[:, first:last] = inner_right[0:8, :]
    rest_rs[0:4, HALF + first : HALF + last] = inner_right[8:12, :]
    rest_rs[4:8, first:last] = inner_right[8:12, :]

    def finish(i, carry):
        for b in (i, i + INNER_LO + INNER - 1):
            col = pl.multiple_of(b * LANES, LANES)
            top, rest = right_side_block(up, col, side, side_x, side_y, col)
            rs[:, pl.ds(col, LANES)] = top
            rest_rs[0:4, pl.ds(col + HALF, LANES)] = rest
            rest_rs[4:8, pl.ds(col, LANES)] = rest
        return carry

    lax.fori_loop(0, INNER_LO + 1, finish, 0)

    lane = lax.broadcasted_iota(jnp.int32, (1, LANES), 1)
    start, end = slice(0, LANES), slice(WIDE - LANES, WIDE)
    rs[:, start] = jnp.where(lane < NBR_REACH, rs[:, end], rs[:, start])
    start, end = slice(HALF, HALF + LANES), slice(2 * HALF - LANES, 2 * HALF)
    rest_rs[0:4, start] = jnp.where(lane < NBR_REACH, rest_rs[4:8, end], rest_rs[0:4, start])
    rest_rs[4:5, end] = packed[36:37, 0:LANES]
    for j in range(GROUPS):
        send[j, :, 0:SENT] = rs[:, 0:SENT]
        send[j, :, SENT:] = rest_rs[:, HALF : 2 * HALF]


def band_block(side, weight, col):
    lane = lax.broadcasted_iota(jnp.int32, (1, LANES), 1)
    slot = lax.broadcasted_iota(jnp.int32, (2 * LANES, LANES), 0)
    cells = pl.ds(col, LANES)
    dense = jnp.zeros((2 * LANES, LANES), f32)
    for k in range(SIDES):
        at = side[k : k + 1, cells] + (lane + NBR_REACH)
        dense = dense + jnp.where(slot == at, weight[k : k + 1, cells], 0.0)
    return split(dense)


def band_kernel(left, right, nbr, lap, *refs):
    *matrices, near_side, near_weight, total, side, side_w = refs
    mid = slice(EDGE, EDGE + CELLS)
    for halo, cells in ((left, slice(0, EDGE)), (right, slice(EDGE + CELLS, WIDE))):
        side[0:4, cells] = halo[52:56, 0:EDGE].astype(jnp.int32)
        side[4:6, cells] = halo[52:54, 2 * EDGE :].astype(jnp.int32)
        side_w[0:4, cells] = halo[52:56, EDGE : 2 * EDGE]
        side_w[4:6, cells] = halo[54:56, 2 * EDGE :]
    own = lax.broadcasted_iota(jnp.int32, (1, CELLS), 1)
    side[:, mid] = nbr[...] - NBR_REACH - own
    side_w[:, mid] = lap[...]
    total[...] = jnp.sum(side_w[...], axis=0, keepdims=True)
    near_side[...] = side[:, LANES : (1 + NEAR) * LANES]
    near_weight[...] = side_w[:, LANES : (1 + NEAR) * LANES]
    for part, matrix in enumerate(matrices):

        def block(b, carry):
            col = pl.multiple_of(((part + 1) * NEAR + b + 1) * LANES, LANES)
            matrix[b, :, 0:LANES], matrix[b, :, LANES:] = band_block(side, side_w, col)
            return carry

        lax.fori_loop(0, NEAR, block, 0)


def solve_kernel(
    got, total, to_first, to_second, from_rows, *refs
):
    near_side, near_weight, *matrices = refs[: BANDS + 2]
    out, x, rhs, scaled, parts, others, last, held = refs[BANDS + 2 :]
    for b in range(NEAR):
        held[b, :, 0:LANES], held[b, :, LANES:] = band_block(near_side, near_weight, b * LANES)
    matrices = [held, *matrices]
    modes = GROUPS * ROWS
    lane = lax.broadcasted_iota(jnp.int32, (1, LANES), 1)
    coef_row = jnp.sum(got[:, 4, SENT + HALF - LANES :], axis=0, keepdims=True)
    eye = lax.broadcasted_iota(jnp.int32, (modes, LANES), 0) == lax.broadcasted_iota(
        jnp.int32, (modes, LANES), 1
    )
    coef = jnp.sum(jnp.where(eye, coef_row, 0.0), axis=1, keepdims=True)
    radius = 6.0 * coef / (1.0 + 6.0 * coef)
    steps = [
        1.0 / (1.0 + radius * math.cos(math.pi * (2 * s + 1) / (2.0 * SWEEPS)))
        for s in range(SWEEPS)
    ]
    dot = functools.partial(jnp.dot, preferred_element_type=f32)

    def keep(dst, b, v):
        both = jnp.concatenate(split(pltpu.roll(v, NBR_REACH, 1)), axis=0)
        for d in dst:
            d[b or SOLVED + 1, :, NBR_REACH:] = both[:, NBR_REACH:]
            d[b + 1, :, 0:NBR_REACH] = both[:, 0:NBR_REACH]

    half = WIDE_BLOCKS // 2
    transforms = [jnp.concatenate(split(m[...]), axis=0) for m in (to_first, to_second)]
    for b in range(SOLVED + 1):
        cols = slice(b * LANES, (b + 1) * LANES)
        rest = SENT + b % half * LANES
        levels = jnp.concatenate(
            [
                got[:, :, cols].reshape(GROUPS * 8, LANES),
                got[:, :, rest : rest + LANES].reshape(GROUPS * 8, LANES),
            ],
            axis=0,
        )
        four = dot(transforms[b // half], jnp.concatenate(split(levels), axis=1))
        full = four[:modes, :LANES] + (
            four[modes:, :LANES] + four[:modes, LANES:] + four[modes:, LANES:]
        )
        weight = total[:, cols]
        if b == 0:
            weight = jnp.where(lane < NBR_REACH, total[:, SENT:], weight)
        inverse = 1.0 / (1.0 + coef * weight)
        full = full * inverse
        rhs[b] = full
        scaled[b] = coef * inverse
        full = steps[0] * full
        x[b] = full
        keep((parts, others) if b == 0 else (parts,), b, full)

    def swept(source, sweep, b):
        four = dot(
            jnp.concatenate([source[b], source[b + 1]], axis=1), matrices[(b - 1) // NEAR][(b - 1) % NEAR]
        )
        moved = four[:modes, :LANES] + (
            four[modes:, :LANES] + four[:modes, LANES:] + four[modes:, LANES:]
        )
        return (1.0 - steps[sweep]) * x[b] + steps[sweep] * (rhs[b] + scaled[b] * moved)

    for sweep, source, target in ((1, parts, others), (2, others, parts)):
        for b in range(1, SOLVED + 1):
            fresh = swept(source, sweep, b)
            x[b] = fresh
            keep((target,), b, fresh)
    first = EDGE // LANES
    for i in range(CELLS // LANES):
        both = jnp.concatenate(split(swept(parts, 3, first + i)), axis=0)
        last[i // 2, :, i % 2 * LANES : (i % 2 + 1) * LANES] = both
    back = jnp.concatenate(split(from_rows[...]), axis=0)
    for i in range(CELLS // (2 * LANES)):
        both = dot(back, last[i])
        out[:, 2 * i * LANES : 2 * (i + 1) * LANES] = both[0:ROWS] + both[16 : 16 + ROWS]


def slab_order(matrix):
    groups = matrix.reshape(GROUPS, ROWS, -1)
    main = groups[:, 0:8].reshape(GROUPS * 8, -1)
    pads = (((0, 0), (0, 4), (0, 0)), ((0, 0), (4, 0), (0, 0)))
    return [
        jnp.concatenate([main, jnp.pad(groups[:, 8:12], pad).reshape(GROUPS * 8, -1)], axis=0)
        for pad in pads
    ]


def call(kernel, outs, scratch=(), name=None, spaces="", out_spaces="", vmem=32):
    kinds = {"s": pltpu.SMEM, "h": pltpu.HBM, "v": pltpu.VMEM}
    in_specs = [pl.BlockSpec(memory_space=kinds[k]) for k in spaces]
    shapes = [jax.ShapeDtypeStruct(s, d) for s, d in outs]
    specs = [pl.BlockSpec(memory_space=kinds[k]) for k in out_spaces or "v" * len(outs)]
    if len(outs) == 1:
        shapes, specs = shapes[0], specs[0]
    return pl.pallas_call(
        kernel,
        out_shape=shapes,
        in_specs=in_specs,
        out_specs=specs,
        scratch_shapes=list(scratch),
        name=name,
        compiler_params=pltpu.CompilerParams(vmem_limit_bytes=int(vmem * MIB)),
    )


def per_device(
    fields,
    stencil_index,
    stencil_weight,
    neighbours,
    lap_weight,
    edge_x,
    edge_y,
    to_modes,
    from_modes,
    helm_coef,
):
    patches = lax.axis_size("patch")
    group = lax.axis_index("lev")
    halo = ((HALO_ROWS, FIELD_EDGE), f32)
    buffers = [
        pltpu.VMEM((3, ROWS, FIELD_EDGE), f32),
        pltpu.VMEM((POINTS, 1, EDGE), jnp.int32),
        pltpu.VMEM((POINTS, 1, EDGE), f32),
        pltpu.VMEM((SIDES, EDGE), jnp.int32),
    ] + [pltpu.VMEM((SIDES, EDGE), f32)] * 3
    head, tail, coef_row = call(
        halo_kernel,
        [halo, halo, ((1, LANES), f32)],
        buffers * 2
        + [pltpu.SMEM((ROWS,), f32), pltpu.SemaphoreType.DMA((17,)), pltpu.VMEM(*halo), pltpu.VMEM(*halo)],
        name="halo",
        spaces="s" + 8 * "h",
        out_spaces="hhv",
        vmem=60,
    )(
        group[None], helm_coef, fields, stencil_index, stencil_weight, neighbours, lap_weight,
        edge_x, edge_y,
    )
    left = lax.ppermute(tail, "patch", [(i, (i + 1) % patches) for i in range(patches)])
    right = lax.ppermute(head, "patch", [((i + 1) % patches, i) for i in range(patches)])
    tiles = CELLS // LANES
    packed, slabs, inner, inner_right, side = call(
        inner_kernel,
        [
            ((40, CELLS), f32),
            ((tiles, 40, 2 * LANES), bf16),
            ((40, CELLS), f32),
            ((ROWS, (INNER - 2) * LANES), f32),
            ((SIDES, CELLS), jnp.int32),
        ],
        name="inner",
        spaces=7 * "v",
    )(fields, stencil_index, stencil_weight, neighbours, edge_x, edge_y, coef_row)
    near = (FIELD_EDGE + REACH) // LANES
    new_winds, send = call(
        outer_kernel,
        [((2, ROWS, CELLS), f32), ((GROUPS, 8, SENT + HALF), f32)],
        [
            pltpu.VMEM((2, 40, near * LANES), f32),
            pltpu.VMEM((2, near, 40, 2 * LANES), bf16),
            pltpu.VMEM((40, WIDE + 2 * LANES), f32),
            pltpu.VMEM((SIDES, WIDE), jnp.int32),
            pltpu.VMEM((SIDES, WIDE), f32),
            pltpu.VMEM((SIDES, WIDE), f32),
            pltpu.VMEM((8, WIDE), f32),
            pltpu.VMEM((8, WIDE + HALF), f32),
        ],
        name="outer",
        spaces=11 * "v",
    )(
        packed, slabs, inner, inner_right, left, right, stencil_index, stencil_weight,
        side, edge_x, edge_y,
    )
    bands = ((NEAR, 2 * LANES, 2 * LANES), bf16)
    near = (SIDES, NEAR * LANES)
    *matrices, near_side, near_weight, total = call(
        band_kernel,
        [bands] * BANDS + [(near, jnp.int32), (near, f32), ((1, WIDE), f32)],
        [pltpu.VMEM((SIDES, WIDE), jnp.int32), pltpu.VMEM((SIDES, WIDE), f32)],
        name="band",
        spaces=4 * "v",
    )(left, right, neighbours, lap_weight)
    got = lax.all_to_all(send, "lev", split_axis=0, concat_axis=0, tiled=True)
    to_slabs = [m.T for m in slab_order(to_modes.T)]
    from_rows = lax.dynamic_slice_in_dim(from_modes, group * ROWS, ROWS, 0)
    from_rows = jnp.pad(jnp.tile(from_rows, (1, 2)), ((0, 16 - ROWS), (0, 0)))
    modes = GROUPS * ROWS
    new_height = call(
        solve_kernel,
        [((ROWS, CELLS), f32)],
        [pltpu.VMEM((SOLVED + 1, modes, LANES), f32)] * 3
        + [pltpu.VMEM((SOLVED + 2, 2 * modes, LANES), bf16)] * 2
        + [
            pltpu.VMEM((CELLS // (2 * LANES), 2 * modes, 2 * LANES), bf16),
            pltpu.VMEM(*bands),
        ],
        name="solve",
        spaces=(7 + BANDS) * "v",
    )(got, total, *to_slabs, from_rows, near_side, near_weight, *matrices)
    return new_winds, new_height


def solution(mesh):
    in_specs = (
        P(None, "lev", "patch"),
        P(None, "lev", "patch"),
        P(None, "lev", "patch"),
        P(None, "patch"),
        P(None, "patch"),
        P(None, "patch"),
        P(None, "patch"),
        P(),
        P(),
        P("lev"),
    )
    out_specs = (P(None, "lev", "patch"), P("lev", "patch"))
    return jax.shard_map(
        per_device, mesh=mesh, in_specs=in_specs, out_specs=out_specs, check_vma=False
    )
```
